32 devices in a mesh: view: 8 (over z, x), img: 4 (over y, core).
Axes of the slice: x: 2, y: 2, z: 4, core: 2. Of those that a mesh axis runs over, the one named last changes fastest.
Arguments:
- volume: bfloat16 [128, 128, 2048], P('view', 'img'), may hold values from -6 to 6
- occupied: int32 [8, 4, 16], P('view', 'img'), may hold values from -1 to 15, as said below
- sample_counts: int32 [8, 4, 16], P('view', 'img'), may hold values from 6 to 24, as said below
- depth_order: int32 [8], replicated, may hold values from 0 to 7, each once
- colors: bfloat16 [3, 128], replicated, may hold values from 0.049804688 to 1
- density: bfloat16 [128], replicated, may hold values from 0.0019989014 to 0.039794922
Outputs:
- frame: float32 [4, 128, 2048], P(None, 'img', 'view')
The draws below stay inside these ranges and needn't reach their ends.
Inputs may be any that keep to these rules, and one draw needn't show every extreme that they name: `occupied`: each brick's list names distinct tiles of 0..15 first and then holds -1; a brick lists 16, half, a quarter or an eighth of its tiles (at least 2), and some brick lists all of them. `sample_counts`: every brick has a tile with 24 samples. `depth_order`: A permutation of the bricks along view.
All inputs are finite; a program needn't handle non-finite values.
Results may differ from the reference program's by a relative error of at most 0.0003.
Values may be sent and summed in bfloat16 or wider, within the bound.
A program may use at most 64 MiB of HBM per device.

```python
import math
import jax
import jax.numpy as jnp
from jax import lax

SLICES = 16
ROWS = 32
COLS = 2048
TILE_COLS = 128
SAMPLE_MAX = 24
BINS = 128
SAMPLE_MIN = 6
TILES_DEV = 16
DEPTH = 128
FRAME_ROWS = 128
N_VIEW = 8
N_IMG = 4


def draw_occupied(key, part):
    bricks = N_VIEW * N_IMG
    key_drop, key_full, key_order = jax.random.split(jax.random.fold_in(key, 101), 3)
    halvings = jax.random.randint(key_drop, (bricks,), 0, 4)
    fullest = jax.random.randint(key_full, (), 0, bricks)
    halvings = jnp.where(jnp.arange(bricks) == fullest, 0, halvings)
    listed_count = jnp.maximum(jnp.right_shift(jnp.int32(TILES_DEV), halvings), 2)
    shuffled = jax.vmap(lambda inner: jax.random.permutation(inner, TILES_DEV))(jax.random.split(key_order, bricks))
    chosen = jnp.where(jnp.arange(TILES_DEV)[None, :] < listed_count[:, None], shuffled, -1)
    return chosen.reshape(N_VIEW, N_IMG, TILES_DEV).astype(jnp.int32)


def draw_sample_counts(key, part):
    bricks = N_VIEW * N_IMG
    key_count, key_top = jax.random.split(jax.random.fold_in(key, 202))
    drawn = jax.random.randint(key_count, (bricks, TILES_DEV), SAMPLE_MIN, SAMPLE_MAX + 1)
    topmost = jax.random.randint(key_top, (bricks, 1), 0, TILES_DEV)
    drawn = jnp.where(jnp.arange(TILES_DEV)[None, :] == topmost, SAMPLE_MAX, drawn)
    return drawn.reshape(N_VIEW, N_IMG, TILES_DEV).astype(jnp.int32)


def level_of(stream_key, extent, cuts, low, largest):
    factor_of, own = 1.0, jax.random.fold_in(stream_key, 6)
    for dim, shards_of in cuts:
        steps = jnp.exp(jax.random.uniform(jax.random.fold_in(own, dim), (shards_of,), jnp.float32, low / len(cuts), largest / len(cuts)))
        factor_of = factor_of * jnp.repeat(steps, extent[dim] // shards_of).reshape([-1 if axis == dim else 1 for axis in range(len(extent))])
    return factor_of


def normal_values(own_key, extent, spread, reach, shards=(), held_as=jnp.bfloat16):
    values = jax.random.normal(own_key, extent, jnp.float32) * spread
    if len(shards) > 0:
        values = level_of(own_key, extent, shards, -0.22, 0.18) * values
    return jnp.clip(values, min=-reach, max=reach).astype(held_as)


def setup_inputs(seed: int = 0) -> dict:
    key_list = jax.random.split(jax.random.key(seed), 7)
    volume = normal_values(key_list[0], (DEPTH, FRAME_ROWS, COLS), 1.0, 6.0, ((0, 8), (1, 4)))
    occupied = draw_occupied(jax.random.fold_in(key_list[6], 71), 0)
    sample_counts = draw_sample_counts(jax.random.fold_in(key_list[6], 71), 0)
    depth_order = jax.random.permutation(key_list[3], N_VIEW).astype(jnp.int32)
    colors = jnp.clip(jax.random.uniform(key_list[4], (3, BINS), jnp.float32, 0.049804688, 1.0), 0.049804688, 1.0).astype(jnp.bfloat16)
    density = jnp.clip(jnp.exp(jax.random.uniform(key_list[5], (BINS,), jnp.float32, math.log(0.0019989014), math.log(0.039794922))), 0.0019989014, 0.039794922).astype(jnp.bfloat16)
    return dict(volume=volume, occupied=occupied, sample_counts=sample_counts, depth_order=depth_order, colors=colors, density=density)


def tent(offset):
    return jnp.maximum(0.0, 1.0 - jnp.abs(offset))


def reference(volume, occupied, sample_counts, depth_order, colors, density):
    table = jnp.concatenate([colors, density[None, :]], axis=0)
    zero_slice = jnp.zeros((1, FRAME_ROWS, COLS), volume.dtype)
    padded = jnp.pad(jnp.concatenate([volume, zero_slice], axis=0), ((0, 0), (1, 1), (1, 1)))
    tile_of_column = jnp.arange(COLS, dtype=jnp.int32) // TILE_COLS
    slice_index = jnp.arange(SLICES + 1, dtype=jnp.float32)
    bin_index = jnp.arange(BINS, dtype=jnp.float32)[:, None]
    tile_index = jnp.arange(TILES_DEV, dtype=jnp.int32)

    def march_brick(brick):
        view_pos = (brick // N_IMG).astype(jnp.int32)
        group_pos = (brick % N_IMG).astype(jnp.int32)
        anchor = jnp.zeros((), jnp.int32)
        cube = lax.dynamic_slice(padded, ((view_pos * SLICES).astype(jnp.int32), (group_pos * ROWS).astype(jnp.int32), anchor), (SLICES + 1, ROWS + 2, COLS + 2)).astype(jnp.float32)
        across = (cube[:, 2:, 1:-1] - cube[:, :-2, 1:-1]) * 0.5
        along = (cube[:, 1:-1, 2:] - cube[:, 1:-1, :-2]) * 0.5
        grads = across * across + along * along
        values = cube[:, 1:-1, 1:-1]
        listed = lax.dynamic_slice(occupied, (view_pos, group_pos, anchor), (1, 1, TILES_DEV))[0, 0]
        counted = lax.dynamic_slice(sample_counts, (view_pos, group_pos, anchor), (1, 1, TILES_DEV))[0, 0]
        present = jnp.any(listed[None, :] == tile_index[:, None], axis=1)
        column_count = counted[tile_of_column]
        column_live = present[tile_of_column]
        count_float = column_count.astype(jnp.float32)

        def sample(carry, number):
            paint, cover, remain = carry
            position = (number.astype(jnp.float32) + 1.0) * SLICES / count_float
            weights_z = tent(position[None, :] - slice_index[:, None])
            sampled = jnp.einsum("jc,jrc->rc", weights_z, values, precision=lax.Precision.HIGHEST)
            sampled_grad = jnp.einsum("jc,jrc->rc", weights_z, grads, precision=lax.Precision.HIGHEST)
            levels = jax.nn.sigmoid(sampled) * (BINS - 1)
            lookup = tent(levels.reshape(1, -1) - bin_index).astype(jnp.bfloat16)
            looked = jnp.dot(table, lookup, preferred_element_type=jnp.float32).reshape(4, ROWS, COLS)
            shading = 0.4 + 0.6 * sampled_grad / (1.0 + sampled_grad)
            opacity = 1.0 - jnp.exp(-(looked[3] * SLICES / count_float))
            live_now = jnp.logical_and(number < column_count, column_live)
            opacity = jnp.where(live_now[None, :], opacity, 0.0)
            weight = remain * opacity
            paint = paint + weight * shading * looked[0:3]
            cover = cover + weight
            remain = remain * (1.0 - opacity)
            return (paint, cover, remain), None

        start = (jnp.zeros((3, ROWS, COLS), jnp.float32), jnp.zeros((ROWS, COLS), jnp.float32), jnp.ones((ROWS, COLS), jnp.float32))
        finished, unused = lax.scan(sample, start, jnp.arange(SAMPLE_MAX, dtype=jnp.int32))
        return jnp.concatenate([finished[0], finished[1][None]], axis=0)

    partials = lax.map(march_brick, jnp.arange(N_VIEW * N_IMG, dtype=jnp.int32))
    layers = partials.reshape(N_VIEW, N_IMG, 4, ROWS, COLS).transpose(0, 2, 1, 3, 4).reshape(N_VIEW, 4, FRAME_ROWS, COLS)

    def blend(position, carry):
        image, remain = carry
        chosen = lax.dynamic_index_in_dim(layers, depth_order[position], 0, keepdims=False)
        return image + remain[None] * chosen, remain * (1.0 - chosen[3])

    image, remain = lax.fori_loop(0, N_VIEW, blend, (jnp.zeros((4, FRAME_ROWS, COLS), jnp.float32), jnp.ones((FRAME_ROWS, COLS), jnp.float32)))
    return image
```

```python
import functools
import math

import jax
import jax.numpy as jnp
from jax import lax
from jax.experimental import pallas as pl
from jax.experimental.pallas import tpu as pltpu
from jax.sharding import PartitionSpec as P

LANES = 128
PAD = 8
STRIP = 8
LIMIT = 32767
MOST = 24
GROUP = 8
CHUNK = 4
GRANT = 48 * 2**20


LANE_GATHER = lax.GatherDimensionNumbers(
    offset_dims=(),
    collapsed_slice_dims=(1,),
    start_index_map=(1,),
    operand_batching_dims=(0,),
    start_indices_batching_dims=(0,),
)


def gather_lanes(row, index):
    return lax.gather(
        row, index[..., None], LANE_GATHER, (1, 1), mode=lax.GatherScatterMode.PROMISE_IN_BOUNDS
    )


def flipped(b, mask, bricks):
    result, bit = 0, 1
    while bit < bricks:
        ours, theirs = (b // bit) % 2, (mask // bit) % 2
        result = result + bit * (ours + theirs - 2 * ours * theirs)
        bit *= 2
    return result


def channel_bounds(colors, density, slices):
    cover = 1.0 - jnp.exp2(
        (-1.01 * math.log2(math.e) * slices) * jnp.max(density, axis=1, keepdims=True)
    )
    most = jnp.max(colors, axis=1, keepdims=True)
    return [1.01 * cover * (most[c : c + 1] if c < 3 else 1.0) for c in range(4)]


def lookup_tables(colors, density):
    lane = lax.broadcasted_iota(jnp.int32, (STRIP, LANES), 1)
    here = [jnp.broadcast_to(colors[c : c + 1, :], (STRIP, LANES)) for c in range(3)]
    here.append(jnp.broadcast_to(density, (STRIP, LANES)))
    after = [jnp.where(lane == LANES - 1, 0.0, pltpu.roll(t, LANES - 1, 1)) for t in here]
    return here + after


def fill_band(band):
    source = lax.broadcasted_iota(jnp.int32, band.shape, 0) - LANES
    target = lax.broadcasted_iota(jnp.int32, band.shape, 1)
    band[...] = jnp.where(
        source == target + 1, 0.5, jnp.where(source == target - 1, -0.5, 0.0)
    ).astype(band.dtype)


def along_squares(padded, at, count, tile, band):
    rows = padded.shape[1]
    blocks = [
        padded[at : at + count, :, pl.ds(pl.multiple_of((tile + i) * LANES, LANES), LANES)].reshape(
            count * rows, LANES
        )
        for i in range(3)
    ]
    along = jnp.dot(
        jnp.concatenate(blocks, axis=1), band[...], preferred_element_type=jnp.float32
    ).reshape(count, rows, LANES)
    return along * along, blocks[1].astype(jnp.float32).reshape(count, rows, LANES)


def prepare(tile, padded, first, count, at, band, vals, grads):
    rows = padded.shape[1]
    square, mid = along_squares(padded, at, count, tile, band)
    for j in range(count):
        vals[tile, first + j, PAD : PAD + rows, :] = mid[j] * 0.5
    inner = slice(STRIP, rows - STRIP)
    for j in range(count):
        z = first + j
        across = (
            vals[tile, z, PAD + STRIP + 1 : PAD + rows - STRIP + 1, :]
            - vals[tile, z, PAD + STRIP - 1 : PAD + rows - STRIP - 1, :]
        )
        grads[tile, z, 0:STRIP, :] = square[j, 0:STRIP]
        grads[tile, z, inner, :] = (across * across + square[j, inner]) * (1.0 / 0.6) + (1.0 / 0.6)
        grads[tile, z, rows - STRIP : rows, :] = square[j, rows - STRIP : rows]


def close_edges(tile, low, high, vals, grads):
    slices, rows = grads.shape[1:3]
    here = pl.ds(pl.multiple_of(tile * LANES, LANES), LANES)
    for z in range(slices):
        vals[tile, z, PAD - 1 : PAD, :] = low[z, :, here] * 0.5
        vals[tile, z, PAD + rows : PAD + rows + 1, :] = high[z, :, here] * 0.5
    for z in range(slices):
        for start in (0, rows - STRIP):
            across = (
                vals[tile, z, PAD + start + 1 : PAD + start + 1 + STRIP, :]
                - vals[tile, z, PAD + start - 1 : PAD + start - 1 + STRIP, :]
            )
            grads[tile, z, start : start + STRIP, :] = (
                across * across + grads[tile, z, start : start + STRIP, :]
            ) * (1.0 / 0.6) + (1.0 / 0.6)


def march_tile(tile, samples, shown, tables, vals, grads, bins):
    slices, rows = grads.shape[1] - 1, grads.shape[2]
    inverse = 1.0 / jnp.full((STRIP, LANES), samples.astype(jnp.float32))
    extinct = (-slices * math.log2(math.e)) * inverse
    scaled = lax.div(65535 + samples, samples)
    half = 0.5 * (bins - 1)
    strips = rows // STRIP

    def group(number, carry):
        carry = list(carry)
        for inner in range(GROUP):
            k = number * GROUP + inner
            travel = jnp.minimum(k + 1, samples) * slices
            base = jnp.minimum(lax.shift_right_logical(travel * scaled, 16), slices - 1)
            part = (travel - base * samples).astype(jnp.float32) * inverse
            rate = jnp.where(k < shown, 1.0, 0.0) * extinct
            for strip in range(strips):
                red, green, blue, remain = carry[4 * strip : 4 * strip + 4]
                v0 = vals[tile, base, pl.ds(PAD + strip * STRIP, STRIP), :]
                v1 = vals[tile, base + 1, pl.ds(PAD + strip * STRIP, STRIP), :]
                q0 = grads[tile, base, pl.ds(strip * STRIP, STRIP), :]
                q1 = grads[tile, base + 1, pl.ds(strip * STRIP, STRIP), :]
                level = half * jnp.tanh(v0 + part * (v1 - v0)) + half
                shift = q0 + part * (q1 - q0)
                index = level.astype(jnp.int32)
                frac = level - index.astype(jnp.float32)
                both = jnp.concatenate([frac, 1.0 - frac], axis=0)
                both = both.astype(jnp.bfloat16).astype(jnp.float32)
                upper, lower = both[:STRIP], both[STRIP:]
                found = [gather_lanes(table, index) for table in tables]
                sigma = lower * found[3] + upper * found[7]
                left = remain * jnp.exp2(sigma * rate)
                weight = (remain - left) * (1.0 - 1.0 / shift)
                near = weight * lower
                far = weight * upper
                carry[4 * strip : 4 * strip + 4] = [
                    red + near * found[0] + far * found[4],
                    green + near * found[1] + far * found[5],
                    blue + near * found[2] + far * found[6],
                    left,
                ]
        return tuple(carry)

    zero = jnp.zeros((STRIP, LANES), jnp.float32)
    done = lax.fori_loop(0, MOST // GROUP, group, (zero, zero, zero, zero + 1.0) * strips)
    red, green, blue, remain = [jnp.concatenate(done[c::4], axis=0) for c in range(4)]
    return red, green, blue, 1.0 - remain


def render_kernel(
    bricks,
    groups,
    listed,
    counts,
    order,
    vol,
    colors_ref,
    density_ref,
    out,
    padded,
    nxt,
    low,
    high,
    first,
    last,
    band,
    vals,
    grads,
    mine,
    held,
    load,
    send,
    recv,
    give,
    take,
):
    b, g = lax.axis_index("view"), lax.axis_index("img")
    slices, rows, columns = vol.shape
    tiles = columns // LANES
    per = tiles // bricks
    bins = colors_ref.shape[1]
    barrier = pltpu.get_barrier_semaphore()
    steps = [(-1, 0), (0, 1), (0, -1), (-1, 1), (-1, -1)]

    def exists(vb, vg):
        return jnp.logical_and(
            jnp.logical_and(b + vb >= 0, b + vb < bricks),
            jnp.logical_and(g + vg >= 0, g + vg < groups),
        )

    def greet(vb, vg):
        pl.semaphore_signal(
            barrier, inc=1, device_id=(vb, vg), device_id_type=pl.DeviceIdType.MESH
        )

    met = jnp.int32(bricks - 1)
    for step in range(1, bricks):
        greet(lax.rem(b + step, bricks), g)
    for vb, vg in [(0, 1), (0, -1), (-1, 1), (-1, -1), (1, 1), (1, -1)]:
        here = exists(vb, vg)

        @pl.when(here)
        def _(vb=vb, vg=vg):
            greet(b + vb, g + vg)

        met = met + here.astype(jnp.int32)

    middle = pl.ds(LANES, columns)
    loads = [
        pltpu.make_async_copy(
            vol.at[pl.ds(at, CHUNK)], padded.at[pl.ds(at, CHUNK), :, middle], load.at[at // CHUNK]
        )
        for at in range(0, slices, CHUNK)
    ]
    for copy in loads:
        copy.start()
    for side in (0, LANES + columns):
        padded[:, :, side : side + LANES] = jnp.zeros((slices, rows, LANES), padded.dtype)
        nxt[:, :, side : side + LANES] = jnp.zeros((1, rows, LANES), nxt.dtype)
    fill_band(band)
    colors = colors_ref[...].astype(jnp.float32)
    density = density_ref[...].astype(jnp.float32)
    tables = lookup_tables(colors, density)
    bounds = channel_bounds(colors, density, slices)
    for copy in loads:
        copy.wait()
    for j in range(slices):
        first[j] = padded[j, 0:STRIP, middle].astype(jnp.float32)[0:1]
        last[j] = padded[j, rows - STRIP : rows, middle].astype(jnp.float32)[STRIP - 1 : STRIP]
    pl.semaphore_wait(barrier, met)

    main, extra = pl.ds(0, slices), pl.ds(slices, 1)
    plan = [
        (vol.at[pl.ds(0, 1)], nxt.at[:, :, middle]),
        (last, low.at[main]),
        (first, high.at[main]),
        (last.at[pl.ds(0, 1)], low.at[extra]),
        (first.at[pl.ds(0, 1)], high.at[extra]),
    ]

    def halo(i):
        (vb, vg), (source, target) = steps[i], plan[i]
        return pltpu.make_async_remote_copy(
            src_ref=source,
            dst_ref=target,
            send_sem=send.at[i],
            recv_sem=recv.at[i],
            device_id=(b + vb, g + vg),
            device_id_type=pl.DeviceIdType.MESH,
        )

    for i, (vb, vg) in enumerate(steps):

        @pl.when(exists(vb, vg))
        def _(i=i):
            halo(i).start()

        @pl.when(jnp.logical_not(exists(-vb, -vg)))
        def _(i=i):
            plan[i][1][...] = jnp.zeros(plan[i][1].shape, plan[i][1].dtype)

    def ready(tile, carry):
        for at in range(0, slices, slices):
            prepare(tile, padded, at, slices, at, band, vals, grads)
        return carry

    lax.fori_loop(0, tiles, ready, 0)

    for i, (vb, vg) in enumerate(steps):

        @pl.when(exists(-vb, -vg))
        def _(i=i):
            halo(i).wait_recv()

    def ready_next(tile, carry):
        prepare(tile, nxt, slices, 1, 0, band, vals, grads)
        return carry

    lax.fori_loop(0, tiles, ready_next, 0)

    scales = [2.0 * LIMIT / bound for bound in bounds]

    def place(i):
        mask, part = bricks - 1 - i // per, i % per
        peer = flipped(b, mask, bricks)
        return mask, part, peer

    def give_away(i):
        mask, part, peer = place(i)
        return pltpu.make_async_remote_copy(
            src_ref=mine.at[peer * per + part],
            dst_ref=held.at[b, part],
            send_sem=give.at[mask, part],
            recv_sem=take.at[mask, part],
            device_id=(peer, g),
            device_id_type=pl.DeviceIdType.MESH,
        )

    def march(i, carry):
        _, part, peer = place(i)
        tile = peer * per + part
        samples = counts[tile]
        live = jnp.int32(0)
        for slot in range(tiles):
            live = jnp.maximum(live, (listed[slot] == tile).astype(jnp.int32))
        close_edges(tile, low, high, vals, grads)
        result = march_tile(tile, samples, live * samples, tables, vals, grads, bins)
        for c, value in enumerate(result):
            code = (value * scales[c] + 0.5).astype(jnp.int32) - LIMIT
            mine[tile, c] = code.astype(jnp.int16)

        @pl.when(jnp.logical_and(i >= 1, i <= (bricks - 1) * per))
        def _():
            give_away(i - 1).start()

        return carry

    lax.fori_loop(0, tiles, march, 0)
    for part in range(per):
        held[b, part] = mine[b * per + part]
    units = [jnp.broadcast_to(bound / (2.0 * LIMIT), (rows, LANES)) for bound in bounds]
    for i, (vb, vg) in enumerate(steps):

        @pl.when(exists(vb, vg))
        def _(i=i):
            halo(i).wait_send()

    for i in range((bricks - 1) * per):
        give_away(i).wait()

    for part in range(per):
        image = [jnp.zeros((rows, LANES), jnp.float32) for _ in range(4)]
        remain = jnp.ones((rows, LANES), jnp.float32)
        for position in range(bricks):
            chosen = order[position]
            value = [
                (held[chosen, part, c].astype(jnp.float32) + float(LIMIT)) * units[c]
                for c in range(4)
            ]
            image = [image[c] + remain * value[c] for c in range(4)]
            remain = remain * (1.0 - value[3])
        for c in range(4):
            out[c, :, part * LANES : (part + 1) * LANES] = image[c]


def shards(volume, occupied, sample_counts, depth_order, colors, density):
    slices, rows, columns = volume.shape
    bricks, groups = lax.axis_size("view"), lax.axis_size("img")
    tiles = columns // LANES
    per = tiles // bricks
    vmem = pl.BlockSpec(memory_space=pltpu.VMEM)
    smem = pl.BlockSpec(memory_space=pltpu.SMEM)
    hbm = pl.BlockSpec(memory_space=pltpu.HBM)
    return pl.pallas_call(
        functools.partial(render_kernel, bricks, groups),
        out_shape=jax.ShapeDtypeStruct((4, rows, per * LANES), jnp.float32),
        in_specs=[smem, smem, smem, hbm, vmem, vmem],
        out_specs=vmem,
        scratch_shapes=[
            pltpu.VMEM((slices, rows, columns + 2 * LANES), volume.dtype),
            pltpu.VMEM((1, rows, columns + 2 * LANES), volume.dtype),
            pltpu.VMEM((slices + 1, 1, columns), jnp.float32),
            pltpu.VMEM((slices + 1, 1, columns), jnp.float32),
            pltpu.VMEM((slices, 1, columns), jnp.float32),
            pltpu.VMEM((slices, 1, columns), jnp.float32),
            pltpu.VMEM((3 * LANES, LANES), jnp.bfloat16),
            pltpu.VMEM((tiles, slices + 1, rows + 2 * PAD, LANES), jnp.float32),
            pltpu.VMEM((tiles, slices + 1, rows, LANES), jnp.float32),
            pltpu.VMEM((tiles, 4, rows, LANES), jnp.int16),
            pltpu.VMEM((bricks, per, 4, rows, LANES), jnp.int16),
            pltpu.SemaphoreType.DMA((slices // CHUNK,)),
            pltpu.SemaphoreType.DMA((5,)),
            pltpu.SemaphoreType.DMA((5,)),
            pltpu.SemaphoreType.DMA((bricks, per)),
            pltpu.SemaphoreType.DMA((bricks, per)),
        ],
        compiler_params=pltpu.CompilerParams(
            collective_id=0, has_side_effects=True, vmem_limit_bytes=GRANT
        ),
        name="render",
    )(occupied[0, 0], sample_counts[0, 0], depth_order, volume, colors, density[None, :])


def solution(mesh):
    return jax.shard_map(
        shards,
        mesh=mesh,
        in_specs=(
            P("view", "img", None),
            P("view", "img", None),
            P("view", "img", None),
            P(),
            P(),
            P(),
        ),
        out_specs=P(None, "img", "view"),
        check_vma=False,
    )
```

```python
import functools
import math

import jax
import jax.numpy as jnp
from jax import lax
from jax.experimental import pallas as pl
from jax.experimental.pallas import tpu as pltpu
from jax.sharding import PartitionSpec as P

LANES = 128
PAD = 8
STRIP = 8
LIMIT = 32767
MOST = 24
GROUP = 8
ROUNDS = MOST // GROUP
LEVEL = 4096.0
FINE = 65536.0
CHUNK = 4
GRANT = 67043328


LANE_GATHER = lax.GatherDimensionNumbers(
    offset_dims=(),
    collapsed_slice_dims=(1,),
    start_index_map=(1,),
    operand_batching_dims=(0,),
    start_indices_batching_dims=(0,),
)


def gather_lanes(row, index):
    return lax.gather(
        row, index[..., None], LANE_GATHER, (1, 1), mode=lax.GatherScatterMode.PROMISE_IN_BOUNDS
    )


def flipped(b, mask, bricks):
    result, bit = 0, 1
    while bit < bricks:
        ours, theirs = (b // bit) % 2, (mask // bit) % 2
        result = result + bit * (ours + theirs - 2 * ours * theirs)
        bit *= 2
    return result


def channel_bounds(colors, density, slices):
    cover = 1.0 - jnp.exp2(
        (-1.01 * math.log2(math.e) * slices) * jnp.max(density, axis=1, keepdims=True)
    )
    most = jnp.max(colors, axis=1, keepdims=True)
    return [1.01 * cover * (most[c : c + 1] if c < 3 else 1.0) for c in range(4)]


def lookup_tables(colors, density):
    entries = [colors[c : c + 1, :] * LEVEL - 1.0 for c in range(3)] + [density * FINE]
    pairs = []
    for entry in entries:
        here = jnp.broadcast_to(entry, (STRIP, LANES))
        pairs.append(here + pltpu.roll(here, LANES - 1, 1) * (1.0 / LEVEL))
    return pairs


def sample_plan(listed, counts, slices, tiles):
    shape = (MOST, LANES)
    lane = lax.broadcasted_iota(jnp.int32, shape, 1)
    count = jnp.ones(shape, jnp.int32)
    shown = jnp.zeros(shape, jnp.int32)
    for tile in range(tiles):
        count = jnp.where(lane == tile, jnp.maximum(counts[0, 0, tile], 1), count)
    for slot in range(tiles):
        shown = jnp.where(lane == listed[0, 0, slot], count, shown)
    k = lax.broadcasted_iota(jnp.int32, shape, 0)
    travel = jnp.minimum(k + 1, count) * slices
    whole = count.astype(jnp.float32)
    base = ((travel.astype(jnp.float32) + 0.5) / whole).astype(jnp.int32)
    base = jnp.clip(base, 0, slices - 1)
    part = (travel - base * count).astype(jnp.float32) / whole
    rate = jnp.where(k < shown, (-slices * math.log2(math.e) / FINE) / whole, 0.0)
    return jnp.minimum(lane, tiles - 1) * (slices + 1) + base, part, rate


def fill_band(band):
    source = lax.broadcasted_iota(jnp.int32, band.shape, 0) - LANES
    target = lax.broadcasted_iota(jnp.int32, band.shape, 1)
    band[...] = jnp.where(
        source == target + 1, 0.5, jnp.where(source == target - 1, -0.5, 0.0)
    ).astype(band.dtype)


def along_squares(padded, at, count, tile, band):
    rows = padded.shape[1]
    blocks = [
        padded[at : at + count, :, pl.ds(pl.multiple_of((tile + i) * LANES, LANES), LANES)].reshape(
            count * rows, LANES
        )
        for i in range(3)
    ]
    along = jnp.dot(
        jnp.concatenate(blocks, axis=1), band[...], preferred_element_type=jnp.float32
    ).reshape(count, rows, LANES)
    return along * along, blocks[1].astype(jnp.float32).reshape(count, rows, LANES)


def prepare(tile, depth, padded, first, count, at, band, vals, grads):
    rows = padded.shape[1]
    square, mid = along_squares(padded, at, count, tile, band)
    for j in range(count):
        vals[tile * depth + first + j, PAD : PAD + rows, :] = mid[j] * 0.5
    inner = slice(STRIP, rows - STRIP)
    for j in range(count):
        z = first + j
        across = (
            vals[tile * depth + z, PAD + STRIP + 1 : PAD + rows - STRIP + 1, :]
            - vals[tile * depth + z, PAD + STRIP - 1 : PAD + rows - STRIP - 1, :]
        )
        grads[tile * depth + z, 0:STRIP, :] = square[j, 0:STRIP]
        grads[tile * depth + z, inner, :] = (across * across + square[j, inner]) * (1.0 / 0.6) + (1.0 / 0.6)
        grads[tile * depth + z, rows - STRIP : rows, :] = square[j, rows - STRIP : rows]


def close_edges(tile, low, high, vals, grads):
    depth, rows = low.shape[0], grads.shape[1]
    here = pl.ds(pl.multiple_of(tile * LANES, LANES), LANES)
    for z in range(depth):
        vals[tile * depth + z, PAD - 1 : PAD, :] = low[z, :, here] * 0.5
        vals[tile * depth + z, PAD + rows : PAD + rows + 1, :] = high[z, :, here] * 0.5
    for z in range(depth):
        for start in (0, rows - STRIP):
            across = (
                vals[tile * depth + z, PAD + start + 1 : PAD + start + 1 + STRIP, :]
                - vals[tile * depth + z, PAD + start - 1 : PAD + start - 1 + STRIP, :]
            )
            grads[tile * depth + z, start : start + STRIP, :] = (
                across * across + grads[tile * depth + z, start : start + STRIP, :]
            ) * (1.0 / 0.6) + (1.0 / 0.6)


def levels(tile, number, places, parts, vals, grads, half, cells, weights, shades):
    strips = grads.shape[1] // STRIP
    for inner in range(GROUP):
        here = pl.ds(places[number * GROUP + inner, tile], 2)
        part = parts[number * GROUP + inner, tile]
        for strip in range(strips):
            unit = inner * strips + strip
            v = vals[here, PAD + strip * STRIP : PAD + (strip + 1) * STRIP, :]
            q = grads[here, strip * STRIP : (strip + 1) * STRIP, :]
            level = half * jnp.tanh(v[0] + part * (v[1] - v[0])) + half
            shift = q[0] + part * (q[1] - q[0])
            index = level.astype(jnp.int32)
            frac = level - index.astype(jnp.float32)
            cells[number, unit] = index
            weights[number, unit] = jnp.concatenate([frac, 1.0 - frac], axis=0).astype(jnp.bfloat16)
            shades[number, unit] = 1.0 - 1.0 / shift


def composite(tile, number, rates, pairs, cells, weights, shades, carry):
    strips = len(carry)
    for inner in range(GROUP):
        rate = rates[number * GROUP + inner, tile]
        for strip in range(strips):
            unit = inner * strips + strip
            remain, nears, fars, paint = carry[strip]
            index = cells[number, unit]
            both = weights[number, unit].astype(jnp.float32)
            upper, lower = both[:STRIP] * LEVEL, both[STRIP:]
            found = [gather_lanes(pair, index) for pair in pairs]
            whole = [jnp.floor(value) for value in found]
            after = [value - first for value, first in zip(found, whole)]
            sigma = lower * whole[3] + upper * after[3]
            left = remain * jnp.exp2(sigma * rate)
            weight = (remain - left) * shades[number, unit]
            near = weight * lower
            far = weight * upper
            paint = [paint[c] + near * whole[c] + far * after[c] for c in range(3)]
            carry[strip] = (left, nears + near, fars + far, paint)
    return carry


def render_kernel(
    bricks,
    groups,
    listed_in,
    counts_in,
    order_in,
    vol,
    colors_in,
    density_in,
    out,
    listed,
    counts,
    order,
    places,
    parts,
    rates,
    colors_ref,
    density_ref,
    rows_of,
    reals,
    padded,
    nxt,
    low,
    high,
    first,
    last,
    band,
    vals,
    grads,
    cells,
    weights,
    shades,
    mine,
    held,
    small,
    load,
    send,
    recv,
    give,
    take,
):
    b, g = lax.axis_index("view"), lax.axis_index("img")
    slices, rows, columns = vol.shape
    tiles = columns // LANES
    per = tiles // bricks
    bins = colors_in.shape[1]
    barrier = pltpu.get_barrier_semaphore()
    steps = [(-1, 0), (0, 1), (0, -1), (-1, 1), (-1, -1)]

    def exists(vb, vg):
        return jnp.logical_and(
            jnp.logical_and(b + vb >= 0, b + vb < bricks),
            jnp.logical_and(g + vg >= 0, g + vg < groups),
        )

    def greet(vb, vg):
        pl.semaphore_signal(
            barrier, inc=1, device_id=(vb, vg), device_id_type=pl.DeviceIdType.MESH
        )

    met = jnp.int32(bricks - 1)
    for step in range(1, bricks):
        greet(lax.rem(b + step, bricks), g)
    for vb, vg in [(0, 1), (0, -1), (-1, 1), (-1, -1), (1, 1), (1, -1)]:
        here = exists(vb, vg)

        @pl.when(here)
        def _(vb=vb, vg=vg):
            greet(b + vb, g + vg)

        met = met + here.astype(jnp.int32)

    middle = pl.ds(LANES, columns)
    loads = [
        pltpu.make_async_copy(
            vol.at[pl.ds(at, CHUNK)], padded.at[pl.ds(at, CHUNK), :, middle], load.at[at // CHUNK]
        )
        for at in range(0, slices, CHUNK)
    ]
    fetches = [
        pltpu.make_async_copy(source, target, small.at[i])
        for i, (source, target) in enumerate(
            [
                (colors_in, colors_ref),
                (density_in, density_ref),
                (counts_in, counts),
                (listed_in, listed),
                (order_in, order),
            ]
        )
    ]
    for copy in loads + fetches:
        copy.start()
    for side in (0, LANES + columns):
        padded[:, :, side : side + LANES] = jnp.zeros((slices, rows, LANES), padded.dtype)
        nxt[:, :, side : side + LANES] = jnp.zeros((1, rows, LANES), nxt.dtype)
    fill_band(band)
    for copy in fetches:
        copy.wait()
    colors = colors_ref[...].astype(jnp.float32)
    density = density_ref[...].astype(jnp.float32)
    pairs = lookup_tables(colors, density)
    plans = sample_plan(listed, counts, slices, tiles)
    for i, plan_of in enumerate(plans):
        (rows_of if i == 0 else reals.at[i - 1])[...] = plan_of
    bounds = channel_bounds(colors, density, slices)
    for copy in loads:
        copy.wait()
    for j in range(slices):
        first[j] = padded[j, 0:STRIP, middle].astype(jnp.float32)[0:1]
        last[j] = padded[j, rows - STRIP : rows, middle].astype(jnp.float32)[STRIP - 1 : STRIP]
    tables = [
        pltpu.make_async_copy(source, target, small.at[5 + i])
        for i, (source, target) in enumerate(
            [(rows_of, places), (reals.at[0], parts), (reals.at[1], rates)]
        )
    ]
    for copy in tables:
        copy.start()
    pl.semaphore_wait(barrier, met)

    main, extra = pl.ds(0, slices), pl.ds(slices, 1)
    plan = [
        (vol.at[pl.ds(0, 1)], nxt.at[:, :, middle]),
        (last, low.at[main]),
        (first, high.at[main]),
        (last.at[pl.ds(0, 1)], low.at[extra]),
        (first.at[pl.ds(0, 1)], high.at[extra]),
    ]

    def halo(i):
        (vb, vg), (source, target) = steps[i], plan[i]
        return pltpu.make_async_remote_copy(
            src_ref=source,
            dst_ref=target,
            send_sem=send.at[i],
            recv_sem=recv.at[i],
            device_id=(b + vb, g + vg),
            device_id_type=pl.DeviceIdType.MESH,
        )

    for i, (vb, vg) in enumerate(steps):

        @pl.when(exists(vb, vg))
        def _(i=i):
            halo(i).start()

        @pl.when(jnp.logical_not(exists(-vb, -vg)))
        def _(i=i):
            plan[i][1][...] = jnp.zeros(plan[i][1].shape, plan[i][1].dtype)

    def ready(tile, carry):
        for at in range(0, slices, slices):
            prepare(tile, slices + 1, padded, at, slices, at, band, vals, grads)
        return carry

    lax.fori_loop(0, tiles, ready, 0)

    for i, (vb, vg) in enumerate(steps):

        @pl.when(exists(-vb, -vg))
        def _(i=i):
            halo(i).wait_recv()

    for copy in tables:
        copy.wait()

    def ready_next(tile, carry):
        prepare(tile, slices + 1, nxt, slices, 1, 0, band, vals, grads)
        return carry

    lax.fori_loop(0, tiles, ready_next, 0)

    scales = [2.0 * LIMIT / bound for bound in bounds]

    def place(i):
        mask, part = bricks - 1 - i // per, i % per
        peer = flipped(b, mask, bricks)
        return mask, part, peer

    def give_away(i):
        mask, part, peer = place(i)
        return pltpu.make_async_remote_copy(
            src_ref=mine.at[peer * per + part],
            dst_ref=held.at[b, part],
            send_sem=give.at[mask, part],
            recv_sem=take.at[mask, part],
            device_id=(peer, g),
            device_id_type=pl.DeviceIdType.MESH,
        )

    def tile_of(i):
        _, part, peer = place(i)
        return peer * per + part

    half = 0.5 * (bins - 1)

    def closed(tile, carry):
        close_edges(tile, low, high, vals, grads)
        return carry

    lax.fori_loop(0, tiles, closed, 0)
    levels(tile_of(0), 0, places, parts, vals, grads, half, cells, weights, shades)

    def march(i, carry):
        tile = tile_of(i)
        zero = jnp.zeros((STRIP, LANES), jnp.float32)
        state = [(zero + 1.0, zero, zero, [zero] * 3) for _ in range(rows // STRIP)]
        for number in range(ROUNDS):
            if number + 1 < ROUNDS:
                levels(tile, number + 1, places, parts, vals, grads, half, cells, weights, shades)
            state = composite(tile, number, rates, pairs, cells, weights, shades, state)
        after = tile_of(jnp.minimum(i + 1, tiles - 1))
        levels(after, 0, places, parts, vals, grads, half, cells, weights, shades)
        result = []
        for c in range(3):
            paint = [paint[c] + nears + fars * (1.0 / LEVEL) for _, nears, fars, paint in state]
            result.append(jnp.concatenate(paint, axis=0) * (1.0 / LEVEL))
        result.append(1.0 - jnp.concatenate([remain for remain, *_ in state], axis=0))
        for c, value in enumerate(result):
            code = (value * scales[c] + 0.5).astype(jnp.int32) - LIMIT
            mine[tile, c] = code.astype(jnp.int16)

        @pl.when(jnp.logical_and(i >= 1, i <= (bricks - 1) * per))
        def _():
            give_away(i - 1).start()

        return carry

    lax.fori_loop(0, tiles, march, 0)
    for part in range(per):
        held[b, part] = mine[b * per + part]
    units = [jnp.broadcast_to(bound / (2.0 * LIMIT), (rows, LANES)) for bound in bounds]
    for i, (vb, vg) in enumerate(steps):

        @pl.when(exists(vb, vg))
        def _(i=i):
            halo(i).wait_send()

    for i in range((bricks - 1) * per):
        give_away(i).wait()

    for part in range(per):
        image = [jnp.zeros((rows, LANES), jnp.float32) for _ in range(4)]
        remain = jnp.ones((rows, LANES), jnp.float32)
        for position in range(bricks):
            chosen = order[position]
            value = [
                (held[chosen, part, c].astype(jnp.float32) + float(LIMIT)) * units[c]
                for c in range(4)
            ]
            image = [image[c] + remain * value[c] for c in range(4)]
            remain = remain * (1.0 - value[3])
        for c in range(4):
            out[c, :, part * LANES : (part + 1) * LANES] = image[c]


def shards(volume, occupied, sample_counts, depth_order, colors, density):
    slices, rows, columns = volume.shape
    bricks, groups = lax.axis_size("view"), lax.axis_size("img")
    tiles = columns // LANES
    per = tiles // bricks
    vmem = pl.BlockSpec(memory_space=pltpu.VMEM)
    hbm = pl.BlockSpec(memory_space=pltpu.HBM)
    return pl.pallas_call(
        functools.partial(render_kernel, bricks, groups),
        out_shape=jax.ShapeDtypeStruct((4, rows, per * LANES), jnp.float32),
        in_specs=[hbm] * 6,
        out_specs=vmem,
        scratch_shapes=[
            pltpu.SMEM(occupied.shape, jnp.int32),
            pltpu.SMEM(sample_counts.shape, jnp.int32),
            pltpu.SMEM(depth_order.shape, jnp.int32),
            pltpu.SMEM((MOST, LANES), jnp.int32),
            pltpu.SMEM((MOST, LANES), jnp.float32),
            pltpu.SMEM((MOST, LANES), jnp.float32),
            pltpu.VMEM(colors.shape, colors.dtype),
            pltpu.VMEM((1, density.shape[0]), density.dtype),
            pltpu.VMEM((MOST, LANES), jnp.int32),
            pltpu.VMEM((2, MOST, LANES), jnp.float32),
            pltpu.VMEM((slices, rows, columns + 2 * LANES), volume.dtype),
            pltpu.VMEM((1, rows, columns + 2 * LANES), volume.dtype),
            pltpu.VMEM((slices + 1, 1, columns), jnp.float32),
            pltpu.VMEM((slices + 1, 1, columns), jnp.float32),
            pltpu.VMEM((slices, 1, columns), jnp.float32),
            pltpu.VMEM((slices, 1, columns), jnp.float32),
            pltpu.VMEM((3 * LANES, LANES), jnp.bfloat16),
            pltpu.VMEM((tiles * (slices + 1), rows + 2 * PAD, LANES), jnp.float32),
            pltpu.VMEM((tiles * (slices + 1), rows, LANES), jnp.float32),
            pltpu.VMEM((ROUNDS, GROUP * (rows // STRIP), STRIP, LANES), jnp.int32),
            pltpu.VMEM((ROUNDS, GROUP * (rows // STRIP), 2 * STRIP, LANES), jnp.bfloat16),
            pltpu.VMEM((ROUNDS, GROUP * (rows // STRIP), STRIP, LANES), jnp.float32),
            pltpu.VMEM((tiles, 4, rows, LANES), jnp.int16),
            pltpu.VMEM((bricks, per, 4, rows, LANES), jnp.int16),
            pltpu.SemaphoreType.DMA((8,)),
            pltpu.SemaphoreType.DMA((slices // CHUNK,)),
            pltpu.SemaphoreType.DMA((5,)),
            pltpu.SemaphoreType.DMA((5,)),
            pltpu.SemaphoreType.DMA((bricks, per)),
            pltpu.SemaphoreType.DMA((bricks, per)),
        ],
        compiler_params=pltpu.CompilerParams(
            collective_id=0, has_side_effects=True, vmem_limit_bytes=GRANT
        ),
        name="render",
    )(occupied, sample_counts, depth_order, volume, colors, density[None, :])


def solution(mesh):
    return jax.shard_map(
        shards,
        mesh=mesh,
        in_specs=(
            P("view", "img", None),
            P("view", "img", None),
            P("view", "img", None),
            P(),
            P(),
            P(),
        ),
        out_specs=P(None, "img", "view"),
        check_vma=False,
    )
```

```python
import functools
import math

import jax
import jax.numpy as jnp
from jax import lax
from jax.experimental import pallas as pl
from jax.experimental.pallas import tpu as pltpu
from jax.sharding import PartitionSpec as P

LANES = 128
PAD = 8
STRIP = 8
LIMIT = 32767
MOST = 24
GROUP = 8
ROUNDS = MOST // GROUP
LEVEL = 4096.0
FINE = 65536.0
CHUNK = 4
QUARTERS = 4
AHEAD = 2
GRANT = 67043328


LANE_GATHER = lax.GatherDimensionNumbers(
    offset_dims=(),
    collapsed_slice_dims=(1,),
    start_index_map=(1,),
    operand_batching_dims=(0,),
    start_indices_batching_dims=(0,),
)


def gather_lanes(row, index):
    return lax.gather(
        row, index[..., None], LANE_GATHER, (1, 1), mode=lax.GatherScatterMode.PROMISE_IN_BOUNDS
    )


def flipped(b, mask, bricks):
    result, bit = 0, 1
    while bit < bricks:
        ours, theirs = (b // bit) % 2, (mask // bit) % 2
        result = result + bit * (ours + theirs - 2 * ours * theirs)
        bit *= 2
    return result


def spread_circles(bricks):
    known, circles = 1, []
    while known < bricks - 1:
        circles.append(known)
        known += known
    return circles


def channel_bounds(colors, density, slices):
    cover = 1.0 - jnp.exp2(
        (-1.01 * math.log2(math.e) * slices) * jnp.max(density, axis=1, keepdims=True)
    )
    most = jnp.max(colors, axis=1, keepdims=True)
    return [1.01 * cover * (most[c : c + 1] if c < 3 else 1.0) for c in range(4)]


def lookup_tables(colors, density):
    entries = [colors[c : c + 1, :] * LEVEL - 1.0 for c in range(3)] + [density * FINE]
    pairs = []
    for entry in entries:
        here = jnp.broadcast_to(entry, (STRIP, LANES))
        pairs.append(here + pltpu.roll(here, LANES - 1, 1) * (1.0 / LEVEL))
    return pairs


def sample_plan(listed, counts, slices, tiles):
    shape = (MOST, LANES)
    lane = lax.broadcasted_iota(jnp.int32, shape, 1)
    count = jnp.ones(shape, jnp.int32)
    shown = jnp.zeros(shape, jnp.int32)
    for tile in range(tiles):
        count = jnp.where(lane == tile, jnp.maximum(counts[0, 0, tile], 1), count)
    for slot in range(tiles):
        shown = jnp.where(lane == listed[0, 0, slot], count, shown)
    k = lax.broadcasted_iota(jnp.int32, shape, 0)
    travel = jnp.minimum(k + 1, count) * slices
    whole = count.astype(jnp.float32)
    base = ((travel.astype(jnp.float32) + 0.5) / whole).astype(jnp.int32)
    base = jnp.clip(base, 0, slices - 1)
    part = (travel - base * count).astype(jnp.float32) / whole
    rate = jnp.where(k < shown, (-slices * math.log2(math.e) / FINE) / whole, 0.0)
    return jnp.minimum(lane, tiles - 1) * (slices + 1) + base, part, rate


def fill_band(band):
    source = lax.broadcasted_iota(jnp.int32, band.shape, 0) - LANES
    target = lax.broadcasted_iota(jnp.int32, band.shape, 1)
    band[...] = jnp.where(
        source == target + 1, 0.5, jnp.where(source == target - 1, -0.5, 0.0)
    ).astype(band.dtype)


def along_squares(padded, at, count, tile, band):
    rows = padded.shape[1]
    blocks = [
        padded[
            pl.ds(at, count), :, pl.ds(pl.multiple_of((tile + i) * LANES, LANES), LANES)
        ].reshape(count * rows, LANES)
        for i in range(3)
    ]
    along = jnp.dot(
        jnp.concatenate(blocks, axis=1), band[...], preferred_element_type=jnp.float32
    ).reshape(count, rows, LANES)
    return along * along, blocks[1].astype(jnp.float32).reshape(count, rows, LANES)


def prepare(tile, depth, padded, first, count, at, shift, band, vals, grads, squares):
    rows = padded.shape[1]
    square, mid = along_squares(padded, at, count, tile - shift, band)
    for j in range(count):
        vals[tile * depth + first + j, PAD : PAD + rows, :] = mid[j] * 0.5
    inner = slice(STRIP, rows - STRIP)
    for j in range(count):
        z = first + j
        across = (
            vals[tile * depth + z, PAD + STRIP + 1 : PAD + rows - STRIP + 1, :]
            - vals[tile * depth + z, PAD + STRIP - 1 : PAD + rows - STRIP - 1, :]
        )
        squares[tile * depth + z, 0:STRIP, :] = square[j, 0:STRIP]
        grads[tile * depth + z, inner, :] = (across * across + square[j, inner]) * (1.0 / 0.6) + (1.0 / 0.6)
        squares[tile * depth + z, STRIP : 2 * STRIP, :] = square[j, rows - STRIP : rows]


def close_edges(tile, low, high, vals, grads, squares):
    depth, rows = low.shape[0], grads.shape[1]
    here = pl.ds(pl.multiple_of(tile * LANES, LANES), LANES)
    for z in range(depth):
        vals[tile * depth + z, PAD - 1 : PAD, :] = low[z, :, here] * 0.5
        vals[tile * depth + z, PAD + rows : PAD + rows + 1, :] = high[z, :, here] * 0.5
    for z in range(depth):
        for side, start in ((0, 0), (STRIP, rows - STRIP)):
            across = (
                vals[tile * depth + z, PAD + start + 1 : PAD + start + 1 + STRIP, :]
                - vals[tile * depth + z, PAD + start - 1 : PAD + start - 1 + STRIP, :]
            )
            grads[tile * depth + z, start : start + STRIP, :] = (
                across * across + squares[tile * depth + z, side : side + STRIP, :]
            ) * (1.0 / 0.6) + (1.0 / 0.6)


def levels(tile, number, places, parts, vals, grads, half, cells, weights, shades):
    strips = grads.shape[1] // STRIP
    for inner in range(GROUP):
        here = pl.ds(places[number * GROUP + inner, tile], 2)
        part = parts[number * GROUP + inner, tile]
        for strip in range(strips):
            unit = inner * strips + strip
            v = vals[here, PAD + strip * STRIP : PAD + (strip + 1) * STRIP, :]
            q = grads[here, strip * STRIP : (strip + 1) * STRIP, :]
            level = half * jnp.tanh(v[0] + part * (v[1] - v[0])) + half
            shift = q[0] + part * (q[1] - q[0])
            index = level.astype(jnp.int32)
            frac = level - index.astype(jnp.float32)
            cells[number, unit] = index
            weights[number, unit] = jnp.concatenate([frac, 1.0 - frac], axis=0).astype(jnp.bfloat16)
            shades[number, unit] = 1.0 - 1.0 / shift


def composite(tile, number, rates, pairs, cells, weights, shades, carry):
    strips = len(carry)
    for inner in range(GROUP):
        rate = rates[number * GROUP + inner, tile]
        for strip in range(strips):
            unit = inner * strips + strip
            remain, nears, fars, paint = carry[strip]
            index = cells[number, unit]
            both = weights[number, unit].astype(jnp.float32)
            upper, lower = both[:STRIP] * LEVEL, both[STRIP:]
            found = [gather_lanes(pair, index) for pair in pairs]
            whole = [jnp.floor(value) for value in found]
            after = [value - first for value, first in zip(found, whole)]
            sigma = lower * whole[3] + upper * after[3]
            left = remain * jnp.exp2(sigma * rate)
            weight = (remain - left) * shades[number, unit]
            near = weight * lower
            far = weight * upper
            paint = [paint[c] + near * whole[c] + far * after[c] for c in range(3)]
            carry[strip] = (left, nears + near, fars + far, paint)
    return carry


def render_kernel(
    bricks,
    groups,
    listed_in,
    counts_in,
    order_in,
    vol,
    colors_in,
    density_in,
    out,
    listed,
    counts,
    order,
    places,
    parts,
    rates,
    colors_ref,
    density_ref,
    rows_of,
    reals,
    padded,
    nxt,
    low,
    high,
    first,
    last,
    band,
    vals,
    grads,
    squares,
    cells,
    weights,
    shades,
    mine,
    held,
    small,
    load,
    send,
    recv,
    give,
    take,
    wider,
):
    b, g = lax.axis_index("view"), lax.axis_index("img")
    slices, rows, columns = vol.shape
    tiles = columns // LANES
    per = tiles // bricks
    bins = colors_in.shape[1]
    barrier = pltpu.get_barrier_semaphore()
    circles = spread_circles(bricks)
    steps = [(-1, 0), (0, 1), (0, -1), (-1, 1), (-1, -1)]

    def exists(vb, vg):
        return jnp.logical_and(
            jnp.logical_and(b + vb >= 0, b + vb < bricks),
            jnp.logical_and(g + vg >= 0, g + vg < groups),
        )

    def greet(semaphore, vb, vg):
        pl.semaphore_signal(
            semaphore, inc=1, device_id=(vb, vg), device_id_type=pl.DeviceIdType.MESH
        )

    met = jnp.int32(0)
    for vb, vg in steps + [(1, 0), (1, 1), (1, -1)]:
        here = exists(vb, vg)

        @pl.when(here)
        def _(vb=vb, vg=vg):
            greet(barrier, b + vb, g + vg)

        met = met + here.astype(jnp.int32)

    def spread(i):
        for vb in (-circles[i], circles[i]):

            @pl.when(exists(vb, 0))
            def _(vb=vb):
                greet(wider.at[i], b + vb, g)

    def gather_in(i):
        sides = [exists(vb, 0).astype(jnp.int32) for vb in (-circles[i], circles[i])]
        pl.semaphore_wait(wider.at[i], sides[0] + sides[1])

    middle = pl.ds(LANES, columns)
    loads = [
        pltpu.make_async_copy(
            vol.at[pl.ds(at, CHUNK)], padded.at[pl.ds(at, CHUNK), :, middle], load.at[at // CHUNK]
        )
        for at in range(0, slices, CHUNK)
    ]
    fetches = [
        pltpu.make_async_copy(source, target, small.at[i])
        for i, (source, target) in enumerate(
            [
                (colors_in, colors_ref),
                (density_in, density_ref),
                (counts_in, counts),
                (listed_in, listed),
                (order_in, order),
            ]
        )
    ]
    for copy in loads + fetches:
        copy.start()
    for side in (0, LANES + columns):
        padded[:, :, side : side + LANES] = jnp.zeros((slices, rows, LANES), padded.dtype)
    fill_band(band)
    for copy in fetches:
        copy.wait()
    colors = colors_ref[...].astype(jnp.float32)
    density = density_ref[...].astype(jnp.float32)
    pairs = lookup_tables(colors, density)
    plans = sample_plan(listed, counts, slices, tiles)
    for i, plan_of in enumerate(plans):
        (rows_of if i == 0 else reals.at[i - 1])[...] = plan_of
    bounds = channel_bounds(colors, density, slices)
    for copy in loads:
        copy.wait()
    for j in range(slices):
        first[j] = padded[j, 0:STRIP, middle].astype(jnp.float32)[0:1]
        last[j] = padded[j, rows - STRIP : rows, middle].astype(jnp.float32)[STRIP - 1 : STRIP]
    tables = [
        pltpu.make_async_copy(source, target, small.at[5 + i])
        for i, (source, target) in enumerate(
            [(rows_of, places), (reals.at[0], parts), (reals.at[1], rates)]
        )
    ]
    for copy in tables:
        copy.start()
    main, extra = pl.ds(0, slices), pl.ds(slices, 1)
    edges = [nxt, low.at[main], high.at[main], low.at[extra], high.at[extra]]
    for edge, (vb, vg) in zip(edges, steps):

        @pl.when(jnp.logical_not(exists(-vb, -vg)))
        def _(edge=edge):
            edge[...] = jnp.zeros(edge.shape, edge.dtype)

    pl.semaphore_wait(barrier, met)

    blocks = bricks // QUARTERS
    wide = columns // QUARTERS

    def halo(i, turn):
        (vb, vg) = steps[i]
        return lambda receiver: halo_copy(i, vb, vg, flipped(receiver // blocks, turn, QUARTERS))

    def halo_copy(i, vb, vg, quarter):
        some = pl.ds(pl.multiple_of(quarter * wide, LANES), wide)
        start = pl.multiple_of(quarter * wide, LANES)
        source, target = [
            (padded.at[pl.ds(0, 1), :, pl.ds(start, wide + 2 * LANES)], nxt.at[pl.ds(quarter, 1)]),
            (last.at[:, :, some], low.at[main, :, some]),
            (first.at[:, :, some], high.at[main, :, some]),
            (last.at[pl.ds(0, 1), :, some], low.at[extra, :, some]),
            (first.at[pl.ds(0, 1), :, some], high.at[extra, :, some]),
        ][i]
        return pltpu.make_async_remote_copy(
            src_ref=source,
            dst_ref=target,
            send_sem=send.at[i, quarter],
            recv_sem=recv.at[i, quarter],
            device_id=(b + vb, g + vg),
            device_id_type=pl.DeviceIdType.MESH,
        )

    def start_halo(count, carry):
        for i, (vb, vg) in enumerate(steps):

            @pl.when(exists(vb, vg))
            def _(i=i, vb=vb):
                halo(i, QUARTERS - 1 - count)(b + vb).start()

        return carry

    def await_halo(turn):
        for i, (vb, vg) in enumerate(steps):

            @pl.when(exists(-vb, -vg))
            def _(i=i):
                halo(i, turn)(b).wait_recv()

    def ready(tile, carry):
        prepare(tile, slices + 1, padded, 0, slices, 0, 0, band, vals, grads, squares)
        return carry

    def get_ready(leg, carry):
        start_halo(leg, 0)
        lax.fori_loop(leg * around, (leg + 1) * around, ready, 0)
        return carry

    around = tiles // QUARTERS
    for i in range(len(circles)):
        spread(i)
        lax.fori_loop(i, i + 1 if i + 1 < len(circles) else QUARTERS, get_ready, 0)
        if i + 1 < len(circles):
            gather_in(i)

    for copy in tables:
        copy.wait()

    scales = [2.0 * LIMIT / bound for bound in bounds]

    def place(i):
        mask, part = bricks - 1 - i // per, i % per
        peer = flipped(b, mask, bricks)
        return mask, part, peer

    def give_away(i):
        mask, part, peer = place(i)
        return pltpu.make_async_remote_copy(
            src_ref=mine.at[peer * per + part],
            dst_ref=held.at[b, part],
            send_sem=give.at[mask, part],
            recv_sem=take.at[mask, part],
            device_id=(peer, g),
            device_id_type=pl.DeviceIdType.MESH,
        )

    def tile_of(i):
        _, part, peer = place(i)
        return peer * per + part

    half = 0.5 * (bins - 1)

    def close(tile):
        quarter = tile // around
        prepare(
            tile, slices + 1, nxt, slices, 1, quarter, quarter * around, band, vals, grads, squares
        )
        close_edges(tile, low, high, vals, grads, squares)

    await_halo(QUARTERS - 1)
    for i in range(AHEAD):
        close(tile_of(i))
    levels(tile_of(0), 0, places, parts, vals, grads, half, cells, weights, shades)

    def march(i, carry):
        @pl.when(i == 1)
        def _():
            gather_in(len(circles) - 1)

        @pl.when(jnp.logical_and(i >= 1, i <= (bricks - 1) * per))
        def _():
            give_away(i - 1).start()

        @pl.when(jnp.logical_and((i + AHEAD) % around == 0, i + AHEAD < tiles))
        def _():
            await_halo(QUARTERS - 1 - (i + AHEAD) // around)

        tile = tile_of(i)
        zero = jnp.zeros((STRIP, LANES), jnp.float32)
        state = [(zero + 1.0, zero, zero, [zero] * 3) for _ in range(rows // STRIP)]
        for number in range(ROUNDS):
            if number + 1 < ROUNDS:
                levels(tile, number + 1, places, parts, vals, grads, half, cells, weights, shades)
            state = composite(tile, number, rates, pairs, cells, weights, shades, state)
        after = tile_of(jnp.minimum(i + 1, tiles - 1))
        levels(after, 0, places, parts, vals, grads, half, cells, weights, shades)
        close(tile_of(jnp.minimum(i + AHEAD, tiles - 1)))
        result = []
        for c in range(3):
            paint = [paint[c] + nears + fars * (1.0 / LEVEL) for _, nears, fars, paint in state]
            result.append(jnp.concatenate(paint, axis=0) * (1.0 / LEVEL))
        result.append(1.0 - jnp.concatenate([remain for remain, *_ in state], axis=0))
        for c, value in enumerate(result):
            code = (value * scales[c] + 0.5).astype(jnp.int32) - LIMIT
            mine[tile, c] = code.astype(jnp.int16)

        return carry

    lax.fori_loop(0, tiles, march, 0)
    for part in range(per):
        held[b, part] = mine[b * per + part]
    units = [jnp.broadcast_to(bound / (2.0 * LIMIT), (rows, LANES)) for bound in bounds]
    for i, (vb, vg) in enumerate(steps):

        @pl.when(exists(vb, vg))
        def _(i=i, vb=vb):
            for turn in range(QUARTERS):
                halo(i, turn)(b + vb).wait_send()

    for i in range((bricks - 1) * per):
        give_away(i).wait()

    for part in range(per):
        image = [jnp.zeros((rows, LANES), jnp.float32) for _ in range(4)]
        remain = jnp.ones((rows, LANES), jnp.float32)
        for position in range(bricks):
            chosen = order[position]
            value = [
                (held[chosen, part, c].astype(jnp.float32) + float(LIMIT)) * units[c]
                for c in range(4)
            ]
            image = [image[c] + remain * value[c] for c in range(4)]
            remain = remain * (1.0 - value[3])
        for c in range(4):
            out[c, :, part * LANES : (part + 1) * LANES] = image[c]


def shards(volume, occupied, sample_counts, depth_order, colors, density):
    slices, rows, columns = volume.shape
    bricks, groups = lax.axis_size("view"), lax.axis_size("img")
    tiles = columns // LANES
    per = tiles // bricks
    vmem = pl.BlockSpec(memory_space=pltpu.VMEM)
    hbm = pl.BlockSpec(memory_space=pltpu.HBM)
    return pl.pallas_call(
        functools.partial(render_kernel, bricks, groups),
        out_shape=jax.ShapeDtypeStruct((4, rows, per * LANES), jnp.float32),
        in_specs=[hbm] * 6,
        out_specs=vmem,
        scratch_shapes=[
            pltpu.SMEM(occupied.shape, jnp.int32),
            pltpu.SMEM(sample_counts.shape, jnp.int32),
            pltpu.SMEM(depth_order.shape, jnp.int32),
            pltpu.SMEM((MOST, LANES), jnp.int32),
            pltpu.SMEM((MOST, LANES), jnp.float32),
            pltpu.SMEM((MOST, LANES), jnp.float32),
            pltpu.VMEM(colors.shape, colors.dtype),
            pltpu.VMEM((1, density.shape[0]), density.dtype),
            pltpu.VMEM((MOST, LANES), jnp.int32),
            pltpu.VMEM((2, MOST, LANES), jnp.float32),
            pltpu.VMEM((slices, rows, columns + 2 * LANES), volume.dtype),
            pltpu.VMEM((QUARTERS, rows, columns // QUARTERS + 2 * LANES), volume.dtype),
            pltpu.VMEM((slices + 1, 1, columns), jnp.float32),
            pltpu.VMEM((slices + 1, 1, columns), jnp.float32),
            pltpu.VMEM((slices, 1, columns), jnp.float32),
            pltpu.VMEM((slices, 1, columns), jnp.float32),
            pltpu.VMEM((3 * LANES, LANES), jnp.bfloat16),
            pltpu.VMEM((tiles * (slices + 1), rows + 2 * PAD, LANES), jnp.float32),
            pltpu.VMEM((tiles * (slices + 1), rows, LANES), jnp.float32),
            pltpu.VMEM((tiles * (slices + 1), 2 * STRIP, LANES), jnp.float32),
            pltpu.VMEM((ROUNDS, GROUP * (rows // STRIP), STRIP, LANES), jnp.int32),
            pltpu.VMEM((ROUNDS, GROUP * (rows // STRIP), 2 * STRIP, LANES), jnp.bfloat16),
            pltpu.VMEM((ROUNDS, GROUP * (rows // STRIP), STRIP, LANES), jnp.float32),
            pltpu.VMEM((tiles, 4, rows, LANES), jnp.int16),
            pltpu.VMEM((bricks, per, 4, rows, LANES), jnp.int16),
            pltpu.SemaphoreType.DMA((8,)),
            pltpu.SemaphoreType.DMA((slices // CHUNK,)),
            pltpu.SemaphoreType.DMA((5, QUARTERS)),
            pltpu.SemaphoreType.DMA((5, QUARTERS)),
            pltpu.SemaphoreType.DMA((bricks, per)),
            pltpu.SemaphoreType.DMA((bricks, per)),
            pltpu.SemaphoreType.REGULAR((len(spread_circles(bricks)),)),
        ],
        compiler_params=pltpu.CompilerParams(
            collective_id=0, has_side_effects=True, vmem_limit_bytes=GRANT
        ),
        name="render",
    )(occupied, sample_counts, depth_order, volume, colors, density[None, :])


def solution(mesh):
    return jax.shard_map(
        shards,
        mesh=mesh,
        in_specs=(
            P("view", "img", None),
            P("view", "img", None),
            P("view", "img", None),
            P(),
            P(),
            P(),
        ),
        out_specs=P(None, "img", "view"),
        check_vma=False,
    )
```

```python
import functools
import math

import jax
import jax.numpy as jnp
from jax import lax
from jax.experimental import pallas as pl
from jax.experimental.pallas import tpu as pltpu
from jax.sharding import PartitionSpec as P

LANES = 128
PAD = 8
STRIP = 8
LIMIT = 32767
MOST = 24
GROUP = 8
ROUNDS = MOST // GROUP
LEVEL = 4096.0
FINE = 65536.0
CHUNK = 4
QUARTERS = 4
AHEAD = 2
GRANT = 67043328


LANE_GATHER = lax.GatherDimensionNumbers(
    offset_dims=(),
    collapsed_slice_dims=(1,),
    start_index_map=(1,),
    operand_batching_dims=(0,),
    start_indices_batching_dims=(0,),
)


def gather_lanes(row, index):
    return lax.gather(
        row, index[..., None], LANE_GATHER, (1, 1), mode=lax.GatherScatterMode.PROMISE_IN_BOUNDS
    )


def flipped(b, mask, bricks):
    result, bit = 0, 1
    while bit < bricks:
        ours, theirs = (b // bit) % 2, (mask // bit) % 2
        result = result + bit * (ours + theirs - 2 * ours * theirs)
        bit *= 2
    return result


def spread_circles(bricks):
    known, circles = 2, []
    while known < bricks - 1:
        circles.append(known)
        known += known
    return circles


def channel_bounds(colors, density, slices):
    cover = 1.0 - jnp.exp2(
        (-1.01 * math.log2(math.e) * slices) * jnp.max(density, axis=1, keepdims=True)
    )
    most = jnp.max(colors, axis=1, keepdims=True)
    return [1.01 * cover * (most[c : c + 1] if c < 3 else 1.0) for c in range(4)]


def lookup_tables(colors, density):
    pairs = []
    for entry, low in [(colors[c : c + 1, :] * LEVEL, 1.0) for c in range(3)] + [(density * FINE, 0.0)]:
        here = jnp.broadcast_to(entry, (STRIP, LANES))
        pairs.append((here - low) + pltpu.roll(here, LANES - 1, 1) * (1.0 / LEVEL))
    return pairs


def sample_plan(listed, counts, slices, tiles):
    shape = (MOST, LANES)
    lane = lax.broadcasted_iota(jnp.int32, shape, 1)
    count = jnp.ones(shape, jnp.int32)
    shown = jnp.zeros(shape, jnp.int32)
    for tile in range(tiles):
        count = jnp.where(lane == tile, jnp.maximum(counts[0, 0, tile], 1), count)
    for slot in range(tiles):
        shown = jnp.where(lane == listed[0, 0, slot], count, shown)
    k = lax.broadcasted_iota(jnp.int32, shape, 0)
    travel = jnp.minimum(k + 1, count) * slices
    whole = count.astype(jnp.float32)
    base = ((travel.astype(jnp.float32) + 0.5) / whole).astype(jnp.int32)
    base = jnp.clip(base, 0, slices - 1)
    part = (travel - base * count).astype(jnp.float32) / whole
    rate = jnp.where(k < shown, (-slices * math.log2(math.e) / FINE) / whole, 0.0)
    return jnp.minimum(lane, tiles - 1) * (slices + 1) + base, part, rate


def fill_band(band):
    source = lax.broadcasted_iota(jnp.int32, band.shape, 0) - LANES
    target = lax.broadcasted_iota(jnp.int32, band.shape, 1)
    band[...] = jnp.where(
        source == target + 1, 0.5, jnp.where(source == target - 1, -0.5, 0.0)
    ).astype(band.dtype)


def prepare(tile, many, depth, padded, first, count, at, shift, band, vals, grads, squares):
    rows = padded.shape[1]
    blocks = [
        padded[
            pl.ds(at, count), :, pl.ds(pl.multiple_of((tile - shift + i) * LANES, LANES), LANES)
        ].reshape(count * rows, LANES)
        for i in range(many + 2)
    ]
    along = jnp.dot(
        jnp.concatenate(blocks, axis=1),
        band[: (many + 2) * LANES, : many * LANES],
        preferred_element_type=jnp.float32,
    )
    base = tile * depth + first
    for one in range(many):
        square = along[:, one * LANES : (one + 1) * LANES].reshape(count, rows, LANES)
        square = square * square
        mid = blocks[one + 1].astype(jnp.float32).reshape(count, rows, LANES)
        for j in range(count):
            vals[base + one * depth + j, PAD : PAD + rows, :] = mid[j] * 0.5
        inner = slice(STRIP, rows - STRIP)
        for j in range(count):
            row = base + one * depth + j
            across = (
                vals[row, PAD + STRIP + 1 : PAD + rows - STRIP + 1, :]
                - vals[row, PAD + STRIP - 1 : PAD + rows - STRIP - 1, :]
            )
            squares[row, 0:STRIP, :] = square[j, 0:STRIP]
            grads[row, inner, :] = (across * across + square[j, inner]) * (1.0 / 0.6) + (1.0 / 0.6)
            squares[row, STRIP : 2 * STRIP, :] = square[j, rows - STRIP : rows]


def close_edges(tile, low, high, vals, grads, squares):
    depth, rows = low.shape[0], grads.shape[1]
    here = pl.ds(pl.multiple_of(tile * LANES, LANES), LANES)
    for z in range(depth):
        vals[tile * depth + z, PAD - 1 : PAD, :] = low[z, :, here] * 0.5
        vals[tile * depth + z, PAD + rows : PAD + rows + 1, :] = high[z, :, here] * 0.5
    for z in range(depth):
        for side, start in ((0, 0), (STRIP, rows - STRIP)):
            across = (
                vals[tile * depth + z, PAD + start + 1 : PAD + start + 1 + STRIP, :]
                - vals[tile * depth + z, PAD + start - 1 : PAD + start - 1 + STRIP, :]
            )
            grads[tile * depth + z, start : start + STRIP, :] = (
                across * across + squares[tile * depth + z, side : side + STRIP, :]
            ) * (1.0 / 0.6) + (1.0 / 0.6)


def levels(tile, number, places, parts, vals, grads, half, cells, weights, shades):
    strips = grads.shape[1] // STRIP
    for inner in range(GROUP):
        here = pl.ds(places[number * GROUP + inner, tile], 2)
        part = parts[number * GROUP + inner, tile]
        for strip in range(strips):
            unit = inner * strips + strip
            v = vals[here, PAD + strip * STRIP : PAD + (strip + 1) * STRIP, :]
            q = grads[here, strip * STRIP : (strip + 1) * STRIP, :]
            level = half * jnp.tanh(v[0] + part * (v[1] - v[0])) + half
            shift = q[0] + part * (q[1] - q[0])
            index = level.astype(jnp.int32)
            frac = level - index.astype(jnp.float32)
            cells[number, unit] = index
            weights[number, unit] = jnp.concatenate([frac, 1.0 - frac], axis=0).astype(jnp.bfloat16)
            shades[number, unit] = 1.0 - 1.0 / shift


def composite(tile, number, rates, pairs, cells, weights, shades, carry):
    strips = len(carry)
    for inner in range(GROUP):
        rate = rates[number * GROUP + inner, tile]
        for strip in range(strips):
            unit = inner * strips + strip
            remain, fars, paint = carry[strip]
            index = cells[number, unit]
            both = weights[number, unit].astype(jnp.float32)
            upper, lower = both[:STRIP] * LEVEL, both[STRIP:]
            found = [gather_lanes(pair, index) for pair in pairs]
            whole = [jnp.ceil(value) for value in found[:3]] + [jnp.floor(found[3])]
            after = [value - first for value, first in zip(found, whole)]
            sigma = lower * whole[3] + upper * after[3]
            left = remain * jnp.exp2(sigma * rate)
            weight = (remain - left) * shades[number, unit]
            near = weight * lower
            far = weight * upper
            paint = [paint[c] + near * whole[c] + far * after[c] for c in range(3)]
            carry[strip] = (left, fars + far, paint)
    return carry


def render_kernel(
    bricks,
    groups,
    listed_in,
    counts_in,
    vol,
    colors_in,
    density_in,
    held,
    listed,
    counts,
    places,
    parts,
    rates,
    colors_ref,
    density_ref,
    rows_of,
    reals,
    padded,
    nxt,
    low,
    high,
    first,
    last,
    band,
    vals,
    grads,
    squares,
    cells,
    weights,
    shades,
    mine,
    small,
    load,
    send,
    recv,
    give,
    take,
    keep,
    wider,
):
    b, g = lax.axis_index("view"), lax.axis_index("img")
    slices, rows, columns = vol.shape
    tiles = columns // LANES
    per = tiles // bricks
    bins = colors_in.shape[1]
    barrier = pltpu.get_barrier_semaphore()
    circles = spread_circles(bricks)
    steps = [(-1, 0), (0, 1), (0, -1), (-1, 1), (-1, -1)]

    def exists(vb, vg):
        return jnp.logical_and(
            jnp.logical_and(b + vb >= 0, b + vb < bricks),
            jnp.logical_and(g + vg >= 0, g + vg < groups),
        )

    def greet(semaphore, vb, vg):
        pl.semaphore_signal(
            semaphore, inc=1, device_id=(vb, vg), device_id_type=pl.DeviceIdType.MESH
        )

    met = jnp.int32(0)
    for vb, vg in steps + [(1, 0), (1, 1), (1, -1), (2, 0), (-2, 0)]:
        here = exists(vb, vg)

        @pl.when(here)
        def _(vb=vb, vg=vg):
            greet(barrier, b + vb, g + vg)

        met = met + here.astype(jnp.int32)

    def spread(i):
        for vb in (-circles[i], circles[i]):

            @pl.when(exists(vb, 0))
            def _(vb=vb):
                greet(wider.at[i], b + vb, g)

    def gather_in(i):
        sides = [exists(vb, 0).astype(jnp.int32) for vb in (-circles[i], circles[i])]
        pl.semaphore_wait(wider.at[i], sides[0] + sides[1])

    middle = pl.ds(LANES, columns)
    loads = [
        pltpu.make_async_copy(
            vol.at[pl.ds(at, CHUNK)], padded.at[pl.ds(at, CHUNK), :, middle], load.at[at // CHUNK]
        )
        for at in range(0, slices, CHUNK)
    ]
    fetches = [
        pltpu.make_async_copy(source, target, small.at[i])
        for i, (source, target) in enumerate(
            [
                (colors_in, colors_ref),
                (density_in, density_ref),
                (counts_in, counts),
                (listed_in, listed),
            ]
        )
    ]
    for copy in loads + fetches:
        copy.start()
    for side in (0, LANES + columns):
        padded[:, :, side : side + LANES] = jnp.zeros((slices, rows, LANES), padded.dtype)
    fill_band(band)
    for copy in fetches:
        copy.wait()
    colors = colors_ref[...].astype(jnp.float32)
    density = density_ref[...].astype(jnp.float32)
    pairs = lookup_tables(colors, density)
    plans = sample_plan(listed, counts, slices, tiles)
    for i, plan_of in enumerate(plans):
        (rows_of if i == 0 else reals.at[i - 1])[...] = plan_of
    bounds = channel_bounds(colors, density, slices)
    for copy in loads:
        copy.wait()
    for j in range(slices):
        first[j] = padded[j, 0:STRIP, middle].astype(jnp.float32)[0:1]
        last[j] = padded[j, rows - STRIP : rows, middle].astype(jnp.float32)[STRIP - 1 : STRIP]
    tables = [
        pltpu.make_async_copy(source, target, small.at[5 + i])
        for i, (source, target) in enumerate(
            [(rows_of, places), (reals.at[0], parts), (reals.at[1], rates)]
        )
    ]
    for copy in tables:
        copy.start()
    main, extra = pl.ds(0, slices), pl.ds(slices, 1)
    edges = [nxt, low.at[main], high.at[main], low.at[extra], high.at[extra]]
    for edge, (vb, vg) in zip(edges, steps):

        @pl.when(jnp.logical_not(exists(-vb, -vg)))
        def _(edge=edge):
            edge[...] = jnp.zeros(edge.shape, edge.dtype)

    pl.semaphore_wait(barrier, met)

    blocks = bricks // QUARTERS
    wide = columns // QUARTERS

    def halo(i, turn):
        (vb, vg) = steps[i]
        return lambda receiver: halo_copy(i, vb, vg, flipped(receiver // blocks, turn, QUARTERS))

    def halo_copy(i, vb, vg, quarter):
        some = pl.ds(pl.multiple_of(quarter * wide, LANES), wide)
        start = pl.multiple_of(quarter * wide, LANES)
        source, target = [
            (padded.at[pl.ds(0, 1), :, pl.ds(start, wide + 2 * LANES)], nxt.at[pl.ds(quarter, 1)]),
            (last.at[:, :, some], low.at[main, :, some]),
            (first.at[:, :, some], high.at[main, :, some]),
            (last.at[pl.ds(0, 1), :, some], low.at[extra, :, some]),
            (first.at[pl.ds(0, 1), :, some], high.at[extra, :, some]),
        ][i]
        return pltpu.make_async_remote_copy(
            src_ref=source,
            dst_ref=target,
            send_sem=send.at[i, quarter],
            recv_sem=recv.at[i, quarter],
            device_id=(b + vb, g + vg),
            device_id_type=pl.DeviceIdType.MESH,
        )

    def start_halo(count, carry):
        turn = QUARTERS - 1 - count
        for i, (vb, vg) in reversed(list(enumerate(steps))):

            @pl.when(exists(vb, vg))
            def _(i=i, vb=vb):
                halo(i, turn)(b + vb).start()

        return carry

    def await_halo(turn):
        for i, (vb, vg) in enumerate(steps):

            @pl.when(exists(-vb, -vg))
            def _(i=i):
                halo(i, turn)(b).wait_recv()

    def ready(tile, carry):
        prepare(tile * 2, 2, slices + 1, padded, 0, slices, 0, 0, band, vals, grads, squares)
        return carry

    def get_ready(leg, carry):
        start_halo(leg, 0)
        lax.fori_loop(leg * (around // 2), (leg + 1) * (around // 2), ready, 0)
        return carry

    around = tiles // QUARTERS
    spread(0)
    lax.fori_loop(0, QUARTERS - 1, get_ready, 0)
    for i in range(1, len(circles)):
        gather_in(i - 1)
        spread(i)
    lax.fori_loop(QUARTERS - 1, QUARTERS, get_ready, 0)

    for copy in tables:
        copy.wait()

    scales = [2.0 * LIMIT / bound for bound in bounds]

    def place(i):
        turn = i
        mask, part = bricks - 1 - turn // per, turn % per
        peer = flipped(b, mask, bricks)
        return mask, part, peer

    def give_away(i):
        mask, part, peer = place(i)
        return pltpu.make_async_remote_copy(
            src_ref=mine.at[peer * per + part],
            dst_ref=held.at[b, part],
            send_sem=give.at[mask, part],
            recv_sem=take.at[mask, part],
            device_id=(peer, g),
            device_id_type=pl.DeviceIdType.MESH,
        )

    def tile_of(i):
        _, part, peer = place(i)
        return peer * per + part

    half = 0.5 * (bins - 1)

    def close(tile):
        quarter = tile // around
        prepare(
            tile, 1, slices + 1, nxt, slices, 1, quarter, quarter * around, band, vals, grads, squares
        )
        close_edges(tile, low, high, vals, grads, squares)

    await_halo(QUARTERS - 1)
    for i in range(AHEAD):
        close(tile_of(i))
    levels(tile_of(0), 0, places, parts, vals, grads, half, cells, weights, shades)

    def march(i, carry):
        @pl.when(i == 1)
        def _():
            gather_in(len(circles) - 1)

        @pl.when(jnp.logical_and(i >= 1, i <= (bricks - 1) * per))
        def _():
            give_away(i - 1).start()

        for first_use, turn in ((around, 2), (2 * around, 1), (3 * around, 0)):

            @pl.when(i + AHEAD == first_use)
            def _(turn=turn):
                await_halo(turn)

        tile = tile_of(i)
        zero = jnp.zeros((STRIP, LANES), jnp.float32)
        state = [(zero + 1.0, zero, [zero] * 3) for _ in range(rows // STRIP)]
        for number in range(ROUNDS):
            if number + 1 < ROUNDS:
                levels(tile, number + 1, places, parts, vals, grads, half, cells, weights, shades)
            state = composite(tile, number, rates, pairs, cells, weights, shades, state)
        after = tile_of(jnp.minimum(i + 1, tiles - 1))
        levels(after, 0, places, parts, vals, grads, half, cells, weights, shades)
        close(tile_of(jnp.minimum(i + AHEAD, tiles - 1)))
        result = []
        for c in range(3):
            paint = [paint[c] + fars for _, fars, paint in state]
            result.append(jnp.concatenate(paint, axis=0) * (1.0 / LEVEL))
        result.append(1.0 - jnp.concatenate([remain for remain, *_ in state], axis=0))
        for c, value in enumerate(result):
            code = (value * scales[c] + 0.5).astype(jnp.int32) - LIMIT
            mine[tile, c] = code.astype(jnp.int16)

        return carry

    lax.fori_loop(0, tiles, march, 0)
    own = [
        pltpu.make_async_copy(mine.at[b * per + part], held.at[b, part], keep.at[part])
        for part in range(per)
    ]
    for copy in own:
        copy.start()
    for i, (vb, vg) in enumerate(steps):

        @pl.when(exists(vb, vg))
        def _(i=i, vb=vb):
            for turn in range(QUARTERS):
                halo(i, turn)(b + vb).wait_send()

    for copy in own:
        copy.wait()
    for i in range((bricks - 1) * per):
        give_away(i).wait()


def blend_kernel(
    slices, order_in, held_in, colors_in, density_in, out, order, held, colors, density, done, load, save
):
    bricks, per, _, rows, _ = held.shape
    smalls = [(order_in, order), (colors_in, colors), (density_in, density)]
    smalls = [
        pltpu.make_async_copy(source, target, load.at[per + i])
        for i, (source, target) in enumerate(smalls)
    ]
    loads = [
        pltpu.make_async_copy(held_in.at[:, part], held.at[:, part], load.at[part])
        for part in range(per)
    ]
    for copy in smalls + loads:
        copy.start()
    for copy in smalls:
        copy.wait()
    bounds = channel_bounds(
        colors[...].astype(jnp.float32), density[...].astype(jnp.float32), slices
    )
    units = [jnp.broadcast_to(bound / (2.0 * LIMIT), (rows, LANES)) for bound in bounds]
    saves = []
    for part in range(per):
        loads[part].wait()
        image = [jnp.zeros((rows, LANES), jnp.float32) for _ in range(4)]
        remain = jnp.ones((rows, LANES), jnp.float32)
        for position in range(bricks):
            chosen = order[position]
            value = [
                (held[chosen, part, c].astype(jnp.float32) + float(LIMIT)) * units[c]
                for c in range(4)
            ]
            image = [image[c] + remain * value[c] for c in range(4)]
            remain = remain * (1.0 - value[3])
        for c in range(4):
            done[part, c] = image[c]
        saves.append(
            pltpu.make_async_copy(
                done.at[part], out.at[:, :, part * LANES : (part + 1) * LANES], save.at[part]
            )
        )
        saves[-1].start()
    for copy in saves:
        copy.wait()


def shards(volume, occupied, sample_counts, depth_order, colors, density):
    slices, rows, columns = volume.shape
    bricks, groups = lax.axis_size("view"), lax.axis_size("img")
    tiles = columns // LANES
    per = tiles // bricks
    hbm = pl.BlockSpec(memory_space=pltpu.HBM)
    held = pl.pallas_call(
        functools.partial(render_kernel, bricks, groups),
        out_shape=jax.ShapeDtypeStruct((bricks, per, 4, rows, LANES), jnp.int16),
        in_specs=[hbm] * 5,
        out_specs=hbm,
        scratch_shapes=[
            pltpu.SMEM(occupied.shape, jnp.int32),
            pltpu.SMEM(sample_counts.shape, jnp.int32),
            pltpu.SMEM((MOST, LANES), jnp.int32),
            pltpu.SMEM((MOST, LANES), jnp.float32),
            pltpu.SMEM((MOST, LANES), jnp.float32),
            pltpu.VMEM(colors.shape, colors.dtype),
            pltpu.VMEM((1, density.shape[0]), density.dtype),
            pltpu.VMEM((MOST, LANES), jnp.int32),
            pltpu.VMEM((2, MOST, LANES), jnp.float32),
            pltpu.VMEM((slices, rows, columns + 2 * LANES), volume.dtype),
            pltpu.VMEM((QUARTERS, rows, columns // QUARTERS + 2 * LANES), volume.dtype),
            pltpu.VMEM((slices + 1, 1, columns), jnp.float32),
            pltpu.VMEM((slices + 1, 1, columns), jnp.float32),
            pltpu.VMEM((slices, 1, columns), jnp.float32),
            pltpu.VMEM((slices, 1, columns), jnp.float32),
            pltpu.VMEM((4 * LANES, 2 * LANES), jnp.bfloat16),
            pltpu.VMEM((tiles * (slices + 1), rows + 2 * PAD, LANES), jnp.float32),
            pltpu.VMEM((tiles * (slices + 1), rows, LANES), jnp.float32),
            pltpu.VMEM((tiles * (slices + 1), 2 * STRIP, LANES), jnp.float32),
            pltpu.VMEM((ROUNDS, GROUP * (rows // STRIP), STRIP, LANES), jnp.int32),
            pltpu.VMEM((ROUNDS, GROUP * (rows // STRIP), 2 * STRIP, LANES), jnp.bfloat16),
            pltpu.VMEM((ROUNDS, GROUP * (rows // STRIP), STRIP, LANES), jnp.float32),
            pltpu.VMEM((tiles, 4, rows, LANES), jnp.int16),
            pltpu.SemaphoreType.DMA((8,)),
            pltpu.SemaphoreType.DMA((slices // CHUNK,)),
            pltpu.SemaphoreType.DMA((5, QUARTERS)),
            pltpu.SemaphoreType.DMA((5, QUARTERS)),
            pltpu.SemaphoreType.DMA((bricks, per)),
            pltpu.SemaphoreType.DMA((bricks, per)),
            pltpu.SemaphoreType.DMA((per,)),
            pltpu.SemaphoreType.REGULAR((len(spread_circles(bricks)),)),
        ],
        compiler_params=pltpu.CompilerParams(
            collective_id=0, has_side_effects=True, vmem_limit_bytes=GRANT
        ),
        name="render",
    )(occupied, sample_counts, volume, colors, density[None, :])
    return pl.pallas_call(
        functools.partial(blend_kernel, slices),
        out_shape=jax.ShapeDtypeStruct((4, rows, per * LANES), jnp.float32),
        in_specs=[hbm] * 4,
        out_specs=hbm,
        scratch_shapes=[
            pltpu.SMEM(depth_order.shape, jnp.int32),
            pltpu.VMEM(held.shape, held.dtype),
            pltpu.VMEM(colors.shape, colors.dtype),
            pltpu.VMEM((1, density.shape[0]), density.dtype),
            pltpu.VMEM((per, 4, rows, LANES), jnp.float32),
            pltpu.SemaphoreType.DMA((per + 3,)),
            pltpu.SemaphoreType.DMA((per,)),
        ],
        compiler_params=pltpu.CompilerParams(vmem_limit_bytes=GRANT),
        name="blend",
    )(depth_order, held, colors, density[None, :])


def solution(mesh):
    return jax.shard_map(
        shards,
        mesh=mesh,
        in_specs=(
            P("view", "img", None),
            P("view", "img", None),
            P("view", "img", None),
            P(),
            P(),
            P(),
        ),
        out_specs=P(None, "img", "view"),
        check_vma=False,
    )
```

```python
import functools
import math

import jax
import jax.numpy as jnp
from jax import lax
from jax.experimental import pallas as pl
from jax.experimental.pallas import tpu as pltpu
from jax.sharding import PartitionSpec as P

LANES = 128
PAD = 8
STRIP = 8
LIMIT = 32767
MOST = 24
GROUP = 8
ROUNDS = MOST // GROUP
LEVEL = 4096.0
FINE = 65536.0
CHUNK = 4
QUARTERS = 4
AHEAD = 2
GRANT = 67043328


LANE_GATHER = lax.GatherDimensionNumbers(
    offset_dims=(),
    collapsed_slice_dims=(1,),
    start_index_map=(1,),
    operand_batching_dims=(0,),
    start_indices_batching_dims=(0,),
)


def gather_lanes(row, index):
    return lax.gather(
        row, index[..., None], LANE_GATHER, (1, 1), mode=lax.GatherScatterMode.PROMISE_IN_BOUNDS
    )


def flipped(b, mask, bricks):
    result, bit = 0, 1
    while bit < bricks:
        ours, theirs = (b // bit) % 2, (mask // bit) % 2
        result = result + bit * (ours + theirs - 2 * ours * theirs)
        bit *= 2
    return result


def spread_circles(bricks):
    known, circles = 2, []
    while known < bricks - 1:
        circles.append(known)
        known += known
    return circles


def channel_bounds(colors, density, slices):
    cover = 1.0 - jnp.exp2(
        (-1.01 * math.log2(math.e) * slices) * jnp.max(density, axis=1, keepdims=True)
    )
    most = jnp.max(colors, axis=1, keepdims=True)
    return [1.01 * cover * (most[c : c + 1] if c < 3 else 1.0) for c in range(4)]


def lookup_tables(colors, density):
    pairs = []
    for entry, low in [(colors[c : c + 1, :] * LEVEL, 1.0) for c in range(3)] + [(density * FINE, 0.0)]:
        here = jnp.broadcast_to(entry, (STRIP, LANES))
        pairs.append((here - low) + pltpu.roll(here, LANES - 1, 1) * (1.0 / LEVEL))
    return pairs


def sample_plan(listed, counts, slices, tiles):
    shape = (MOST, LANES)
    lane = lax.broadcasted_iota(jnp.int32, shape, 1)
    count = jnp.ones(shape, jnp.int32)
    shown = jnp.zeros(shape, jnp.int32)
    for tile in range(tiles):
        count = jnp.where(lane == tile, jnp.maximum(counts[0, 0, tile], 1), count)
    for slot in range(tiles):
        shown = jnp.where(lane == listed[0, 0, slot], count, shown)
    k = lax.broadcasted_iota(jnp.int32, shape, 0)
    travel = jnp.minimum(k + 1, count) * slices
    whole = count.astype(jnp.float32)
    base = ((travel.astype(jnp.float32) + 0.5) / whole).astype(jnp.int32)
    base = jnp.clip(base, 0, slices - 1)
    part = (travel - base * count).astype(jnp.float32) / whole
    rate = jnp.where(k < shown, (-slices * math.log2(math.e) / FINE) / whole, 0.0)
    return jnp.minimum(lane, tiles - 1) * (slices + 1) + base, part, rate


def fill_band(band):
    source = lax.broadcasted_iota(jnp.int32, band.shape, 0) - LANES
    target = lax.broadcasted_iota(jnp.int32, band.shape, 1)
    band[...] = jnp.where(
        source == target + 1, 0.5, jnp.where(source == target - 1, -0.5, 0.0)
    ).astype(band.dtype)


def prepare(tile, many, depth, padded, first, count, at, shift, band, vals, grads, squares):
    rows = padded.shape[1]
    blocks = [
        padded[
            pl.ds(at, count), :, pl.ds(pl.multiple_of((tile - shift + i) * LANES, LANES), LANES)
        ].reshape(count * rows, LANES)
        for i in range(many + 2)
    ]
    along = jnp.dot(
        jnp.concatenate(blocks, axis=1),
        band[: (many + 2) * LANES, : many * LANES],
        preferred_element_type=jnp.float32,
    )
    base = tile * depth + first
    for one in range(many):
        square = along[:, one * LANES : (one + 1) * LANES].reshape(count, rows, LANES)
        square = square * square
        mid = blocks[one + 1].astype(jnp.float32).reshape(count, rows, LANES)
        for j in range(count):
            vals[base + one * depth + j, PAD : PAD + rows, :] = mid[j] * 0.5
        inner = slice(STRIP, rows - STRIP)
        for j in range(count):
            row = base + one * depth + j
            across = (
                vals[row, PAD + STRIP + 1 : PAD + rows - STRIP + 1, :]
                - vals[row, PAD + STRIP - 1 : PAD + rows - STRIP - 1, :]
            )
            squares[row, 0:STRIP, :] = square[j, 0:STRIP]
            grads[row, inner, :] = (across * across + square[j, inner]) * (1.0 / 0.6) + (1.0 / 0.6)
            squares[row, STRIP : 2 * STRIP, :] = square[j, rows - STRIP : rows]


def close_edges(tile, low, high, vals, grads, squares):
    depth, rows = low.shape[0], grads.shape[1]
    here = pl.ds(pl.multiple_of(tile * LANES, LANES), LANES)
    for z in range(depth):
        vals[tile * depth + z, PAD - 1 : PAD, :] = low[z, :, here] * 0.5
        vals[tile * depth + z, PAD + rows : PAD + rows + 1, :] = high[z, :, here] * 0.5
    for z in range(depth):
        for side, start in ((0, 0), (STRIP, rows - STRIP)):
            across = (
                vals[tile * depth + z, PAD + start + 1 : PAD + start + 1 + STRIP, :]
                - vals[tile * depth + z, PAD + start - 1 : PAD + start - 1 + STRIP, :]
            )
            grads[tile * depth + z, start : start + STRIP, :] = (
                across * across + squares[tile * depth + z, side : side + STRIP, :]
            ) * (1.0 / 0.6) + (1.0 / 0.6)


def levels(tile, number, places, parts, vals, grads, half, cells, weights, shades):
    strips = grads.shape[1] // STRIP
    for inner in range(GROUP):
        here = pl.ds(places[number * GROUP + inner, tile], 2)
        part = parts[number * GROUP + inner, tile]
        for strip in range(strips):
            unit = inner * strips + strip
            v = vals[here, PAD + strip * STRIP : PAD + (strip + 1) * STRIP, :]
            q = grads[here, strip * STRIP : (strip + 1) * STRIP, :]
            level = half * jnp.tanh(v[0] + part * (v[1] - v[0])) + half
            shift = q[0] + part * (q[1] - q[0])
            index = level.astype(jnp.int32)
            frac = level - index.astype(jnp.float32)
            cells[number, unit] = index
            weights[number, unit] = jnp.concatenate([frac, 1.0 - frac], axis=0).astype(jnp.bfloat16)
            shades[number, unit] = 1.0 - 1.0 / shift


def composite(tile, number, rates, pairs, cells, weights, shades, carry):
    strips = len(carry)
    for inner in range(GROUP):
        rate = rates[number * GROUP + inner, tile]
        for strip in range(strips):
            unit = inner * strips + strip
            remain, fars, paint = carry[strip]
            index = cells[number, unit]
            both = weights[number, unit].astype(jnp.float32)
            upper, lower = both[:STRIP] * LEVEL, both[STRIP:]
            found = [gather_lanes(pair, index) for pair in pairs]
            whole = [jnp.ceil(value) for value in found[:3]] + [jnp.floor(found[3])]
            after = [value - first for value, first in zip(found, whole)]
            sigma = lower * whole[3] + upper * after[3]
            left = remain * jnp.exp2(sigma * rate)
            weight = (remain - left) * shades[number, unit]
            near = weight * lower
            far = weight * upper
            paint = [paint[c] + near * whole[c] + far * after[c] for c in range(3)]
            carry[strip] = (left, fars + far, paint)
    return carry


def render_kernel(
    bricks,
    groups,
    listed_in,
    counts_in,
    vol,
    colors_in,
    density_in,
    held,
    listed,
    counts,
    places,
    parts,
    rates,
    colors_ref,
    density_ref,
    rows_of,
    reals,
    padded,
    nxt,
    low,
    high,
    first,
    last,
    band,
    vals,
    grads,
    squares,
    cells,
    weights,
    shades,
    mine,
    small,
    load,
    send,
    recv,
    give,
    take,
    keep,
    wider,
):
    b, g = lax.axis_index("view"), lax.axis_index("img")
    slices, rows, columns = vol.shape
    tiles = columns // LANES
    per = tiles // bricks
    bins = colors_in.shape[1]
    barrier = pltpu.get_barrier_semaphore()
    circles = spread_circles(bricks)
    steps = [(-1, 0), (0, 1), (0, -1), (-1, 1), (-1, -1)]

    def exists(vb, vg):
        return jnp.logical_and(
            jnp.logical_and(b + vb >= 0, b + vb < bricks),
            jnp.logical_and(g + vg >= 0, g + vg < groups),
        )

    def greet(semaphore, vb, vg):
        pl.semaphore_signal(
            semaphore, inc=1, device_id=(vb, vg), device_id_type=pl.DeviceIdType.MESH
        )

    met = jnp.int32(0)
    for vb, vg in steps + [(1, 0), (1, 1), (1, -1), (2, 0), (-2, 0)]:
        here = exists(vb, vg)

        @pl.when(here)
        def _(vb=vb, vg=vg):
            greet(barrier, b + vb, g + vg)

        met = met + here.astype(jnp.int32)

    def spread(i):
        for vb in (-circles[i], circles[i]):

            @pl.when(exists(vb, 0))
            def _(vb=vb):
                greet(wider.at[i], b + vb, g)

    def gather_in(i):
        sides = [exists(vb, 0).astype(jnp.int32) for vb in (-circles[i], circles[i])]
        pl.semaphore_wait(wider.at[i], sides[0] + sides[1])

    middle = pl.ds(LANES, columns)
    loads = [
        pltpu.make_async_copy(
            vol.at[pl.ds(at, CHUNK)], padded.at[pl.ds(at, CHUNK), :, middle], load.at[at // CHUNK]
        )
        for at in range(0, slices, CHUNK)
    ]
    fetches = [
        pltpu.make_async_copy(source, target, small.at[i])
        for i, (source, target) in enumerate(
            [
                (colors_in, colors_ref),
                (density_in, density_ref),
                (counts_in, counts),
                (listed_in, listed),
            ]
        )
    ]
    for copy in loads + fetches:
        copy.start()
    for side in (0, LANES + columns):
        padded[:, :, side : side + LANES] = jnp.zeros((slices, rows, LANES), padded.dtype)
    fill_band(band)
    for copy in fetches:
        copy.wait()
    colors = colors_ref[...].astype(jnp.float32)
    density = density_ref[...].astype(jnp.float32)
    pairs = lookup_tables(colors, density)
    plans = sample_plan(listed, counts, slices, tiles)
    for i, plan_of in enumerate(plans):
        (rows_of if i == 0 else reals.at[i - 1])[...] = plan_of
    bounds = channel_bounds(colors, density, slices)
    for copy in loads:
        copy.wait()
    for j in range(slices):
        first[j] = padded[j, 0:STRIP, middle].astype(jnp.float32)[0:1]
        last[j] = padded[j, rows - STRIP : rows, middle].astype(jnp.float32)[STRIP - 1 : STRIP]
    tables = [
        pltpu.make_async_copy(source, target, small.at[5 + i])
        for i, (source, target) in enumerate(
            [(rows_of, places), (reals.at[0], parts), (reals.at[1], rates)]
        )
    ]
    for copy in tables:
        copy.start()
    main, extra = pl.ds(0, slices), pl.ds(slices, 1)
    edges = [nxt, low.at[main], high.at[main], low.at[extra], high.at[extra]]
    for edge, (vb, vg) in zip(edges, steps):

        @pl.when(jnp.logical_not(exists(-vb, -vg)))
        def _(edge=edge):
            edge[...] = jnp.zeros(edge.shape, edge.dtype)

    pl.semaphore_wait(barrier, met)

    blocks = bricks // QUARTERS
    wide = columns // QUARTERS

    def halo(i, turn):
        (vb, vg) = steps[i]
        return lambda receiver: halo_copy(i, vb, vg, flipped(receiver // blocks, turn, QUARTERS))

    def halo_copy(i, vb, vg, quarter):
        some = pl.ds(pl.multiple_of(quarter * wide, LANES), wide)
        start = pl.multiple_of(quarter * wide, LANES)
        source, target = [
            (padded.at[pl.ds(0, 1), :, pl.ds(start, wide + 2 * LANES)], nxt.at[pl.ds(quarter, 1)]),
            (last.at[:, :, some], low.at[main, :, some]),
            (first.at[:, :, some], high.at[main, :, some]),
            (last.at[pl.ds(0, 1), :, some], low.at[extra, :, some]),
            (first.at[pl.ds(0, 1), :, some], high.at[extra, :, some]),
        ][i]
        return pltpu.make_async_remote_copy(
            src_ref=source,
            dst_ref=target,
            send_sem=send.at[i, quarter],
            recv_sem=recv.at[i, quarter],
            device_id=(b + vb, g + vg),
            device_id_type=pl.DeviceIdType.MESH,
        )

    def start_halo(count, carry):
        turn = QUARTERS - 1 - count
        for i, (vb, vg) in reversed(list(enumerate(steps))):

            @pl.when(exists(vb, vg))
            def _(i=i, vb=vb):
                halo(i, turn)(b + vb).start()

        return carry

    def await_halo(turn):
        for i, (vb, vg) in enumerate(steps):

            @pl.when(exists(-vb, -vg))
            def _(i=i):
                halo(i, turn)(b).wait_recv()

    def ready(tile, carry):
        prepare(tile * 2, 2, slices + 1, padded, 0, slices, 0, 0, band, vals, grads, squares)
        return carry

    def get_ready(leg, carry):
        start_halo(leg, 0)
        lax.fori_loop(leg * (around // 2), (leg + 1) * (around // 2), ready, 0)
        return carry

    around = tiles // QUARTERS
    spread(0)
    lax.fori_loop(0, QUARTERS - 1, get_ready, 0)
    for i in range(1, len(circles)):
        gather_in(i - 1)
        spread(i)
    lax.fori_loop(QUARTERS - 1, QUARTERS, get_ready, 0)

    for copy in tables:
        copy.wait()

    scales = [2.0 * LIMIT / bound / (LEVEL if c < 3 else 1.0) for c, bound in enumerate(bounds)]

    def place(i):
        turn = i
        mask, part = bricks - 1 - turn // per, turn % per
        peer = flipped(b, mask, bricks)
        return mask, part, peer

    def give_away(i):
        mask, part, peer = place(i)
        return pltpu.make_async_remote_copy(
            src_ref=mine.at[peer * per + part],
            dst_ref=held.at[b, part],
            send_sem=give.at[mask, part],
            recv_sem=take.at[mask, part],
            device_id=(peer, g),
            device_id_type=pl.DeviceIdType.MESH,
        )

    def tile_of(i):
        _, part, peer = place(i)
        return peer * per + part

    half = 0.5 * (bins - 1)

    def close(tile):
        quarter = tile // around
        prepare(
            tile, 1, slices + 1, nxt, slices, 1, quarter, quarter * around, band, vals, grads, squares
        )
        close_edges(tile, low, high, vals, grads, squares)

    await_halo(QUARTERS - 1)
    for i in range(AHEAD):
        close(tile_of(i))
    levels(tile_of(0), 0, places, parts, vals, grads, half, cells, weights, shades)

    def march(i, carry):
        @pl.when(i == 1)
        def _():
            gather_in(len(circles) - 1)

        @pl.when(jnp.logical_and(i >= 1, i <= (bricks - 1) * per))
        def _():
            give_away(i - 1).start()

        for first_use, turn in [((QUARTERS - 1 - turn) * around, turn) for turn in range(QUARTERS - 1)]:

            @pl.when(i + AHEAD == first_use)
            def _(turn=turn):
                await_halo(turn)

        tile = tile_of(i)
        zero = jnp.zeros((STRIP, LANES), jnp.float32)
        state = [(zero + 1.0, zero, [zero] * 3) for _ in range(rows // STRIP)]
        for number in range(ROUNDS):
            if number + 1 < ROUNDS:
                levels(tile, number + 1, places, parts, vals, grads, half, cells, weights, shades)
            state = composite(tile, number, rates, pairs, cells, weights, shades, state)
        after = tile_of(jnp.minimum(i + 1, tiles - 1))
        levels(after, 0, places, parts, vals, grads, half, cells, weights, shades)
        close(tile_of(jnp.minimum(i + AHEAD, tiles - 1)))
        result = []
        for c in range(3):
            paint = [paint[c] + fars for _, fars, paint in state]
            result.append(jnp.concatenate(paint, axis=0))
        result.append(1.0 - jnp.concatenate([remain for remain, *_ in state], axis=0))
        for c, value in enumerate(result):
            code = (value * scales[c] + 0.5).astype(jnp.int32) - LIMIT
            mine[tile, c] = code.astype(jnp.int16)

        return carry

    lax.fori_loop(0, tiles, march, 0)
    own = [
        pltpu.make_async_copy(mine.at[b * per + part], held.at[b, part], keep.at[part])
        for part in range(per)
    ]
    for copy in own:
        copy.start()
    for i, (vb, vg) in enumerate(steps):

        @pl.when(exists(vb, vg))
        def _(i=i, vb=vb):
            for turn in range(QUARTERS):
                halo(i, turn)(b + vb).wait_send()

    for copy in own:
        copy.wait()
    for i in range((bricks - 1) * per):
        give_away(i).wait()


def blend_kernel(
    slices, order_in, held_in, colors_in, density_in, out, order, held, colors, density, done, load, save
):
    bricks, per, _, rows, _ = held.shape
    smalls = [(order_in, order), (colors_in, colors), (density_in, density)]
    smalls = [
        pltpu.make_async_copy(source, target, load.at[per + i])
        for i, (source, target) in enumerate(smalls)
    ]
    loads = [
        pltpu.make_async_copy(held_in.at[:, part], held.at[:, part], load.at[part])
        for part in range(per)
    ]
    for copy in smalls + loads:
        copy.start()
    for copy in smalls:
        copy.wait()
    bounds = channel_bounds(
        colors[...].astype(jnp.float32), density[...].astype(jnp.float32), slices
    )
    units = [jnp.broadcast_to(bound / (2.0 * LIMIT), (rows, LANES)) for bound in bounds]
    saves = []
    for part in range(per):
        loads[part].wait()
        image = [jnp.zeros((rows, LANES), jnp.float32) for _ in range(4)]
        remain = jnp.ones((rows, LANES), jnp.float32)
        for position in range(bricks):
            chosen = order[position]
            value = [
                (held[chosen, part, c].astype(jnp.float32) + float(LIMIT)) * units[c]
                for c in range(4)
            ]
            image = [image[c] + remain * value[c] for c in range(4)]
            remain = remain * (1.0 - value[3])
        for c in range(4):
            done[part, c] = image[c]
        saves.append(
            pltpu.make_async_copy(
                done.at[part], out.at[:, :, part * LANES : (part + 1) * LANES], save.at[part]
            )
        )
        saves[-1].start()
    for copy in saves:
        copy.wait()


def shards(volume, occupied, sample_counts, depth_order, colors, density):
    slices, rows, columns = volume.shape
    bricks, groups = lax.axis_size("view"), lax.axis_size("img")
    tiles = columns // LANES
    per = tiles // bricks
    hbm = pl.BlockSpec(memory_space=pltpu.HBM)
    held = pl.pallas_call(
        functools.partial(render_kernel, bricks, groups),
        out_shape=jax.ShapeDtypeStruct((bricks, per, 4, rows, LANES), jnp.int16),
        in_specs=[hbm] * 5,
        out_specs=hbm,
        scratch_shapes=[
            pltpu.SMEM(occupied.shape, jnp.int32),
            pltpu.SMEM(sample_counts.shape, jnp.int32),
            pltpu.SMEM((MOST, LANES), jnp.int32),
            pltpu.SMEM((MOST, LANES), jnp.float32),
            pltpu.SMEM((MOST, LANES), jnp.float32),
            pltpu.VMEM(colors.shape, colors.dtype),
            pltpu.VMEM((1, density.shape[0]), density.dtype),
            pltpu.VMEM((MOST, LANES), jnp.int32),
            pltpu.VMEM((2, MOST, LANES), jnp.float32),
            pltpu.VMEM((slices, rows, columns + 2 * LANES), volume.dtype),
            pltpu.VMEM((QUARTERS, rows, columns // QUARTERS + 2 * LANES), volume.dtype),
            pltpu.VMEM((slices + 1, 1, columns), jnp.float32),
            pltpu.VMEM((slices + 1, 1, columns), jnp.float32),
            pltpu.VMEM((slices, 1, columns), jnp.float32),
            pltpu.VMEM((slices, 1, columns), jnp.float32),
            pltpu.VMEM((4 * LANES, 2 * LANES), jnp.bfloat16),
            pltpu.VMEM((tiles * (slices + 1), rows + 2 * PAD, LANES), jnp.float32),
            pltpu.VMEM((tiles * (slices + 1), rows, LANES), jnp.float32),
            pltpu.VMEM((tiles * (slices + 1), 2 * STRIP, LANES), jnp.float32),
            pltpu.VMEM((ROUNDS, GROUP * (rows // STRIP), STRIP, LANES), jnp.int32),
            pltpu.VMEM((ROUNDS, GROUP * (rows // STRIP), 2 * STRIP, LANES), jnp.bfloat16),
            pltpu.VMEM((ROUNDS, GROUP * (rows // STRIP), STRIP, LANES), jnp.float32),
            pltpu.VMEM((tiles, 4, rows, LANES), jnp.int16),
            pltpu.SemaphoreType.DMA((8,)),
            pltpu.SemaphoreType.DMA((slices // CHUNK,)),
            pltpu.SemaphoreType.DMA((5, QUARTERS)),
            pltpu.SemaphoreType.DMA((5, QUARTERS)),
            pltpu.SemaphoreType.DMA((bricks, per)),
            pltpu.SemaphoreType.DMA((bricks, per)),
            pltpu.SemaphoreType.DMA((per,)),
            pltpu.SemaphoreType.REGULAR((len(spread_circles(bricks)),)),
        ],
        compiler_params=pltpu.CompilerParams(
            collective_id=0, has_side_effects=True, vmem_limit_bytes=GRANT
        ),
        name="render",
    )(occupied, sample_counts, volume, colors, density[None, :])
    return pl.pallas_call(
        functools.partial(blend_kernel, slices),
        out_shape=jax.ShapeDtypeStruct((4, rows, per * LANES), jnp.float32),
        in_specs=[hbm] * 4,
        out_specs=hbm,
        scratch_shapes=[
            pltpu.SMEM(depth_order.shape, jnp.int32),
            pltpu.VMEM(held.shape, held.dtype),
            pltpu.VMEM(colors.shape, colors.dtype),
            pltpu.VMEM((1, density.shape[0]), density.dtype),
            pltpu.VMEM((per, 4, rows, LANES), jnp.float32),
            pltpu.SemaphoreType.DMA((per + 3,)),
            pltpu.SemaphoreType.DMA((per,)),
        ],
        compiler_params=pltpu.CompilerParams(vmem_limit_bytes=GRANT),
        name="blend",
    )(depth_order, held, colors, density[None, :])


def solution(mesh):
    return jax.shard_map(
        shards,
        mesh=mesh,
        in_specs=(
            P("view", "img", None),
            P("view", "img", None),
            P("view", "img", None),
            P(),
            P(),
            P(),
        ),
        out_specs=P(None, "img", "view"),
        check_vma=False,
    )
```
